32 devices in a mesh: alpha: 4 (over z), beta: 4 (over y, core), task: 2 (over x).
Axes of the slice: x: 2, y: 2, z: 4, core: 2. Of those that a mesh axis runs over, the one named last changes fastest.
Arguments:
- vector: float32 [1024, 4096], P('alpha', 'beta'), may hold values from -6 to 6
- op_alpha: float32 [2, 1024, 1024], P('task', 'alpha'), may hold values from -2 to 2, as said below
- op_beta: float32 [2, 4096, 4096], P('task', 'beta'), may hold values from -2 to 2, as said below
- op_weight: float32 [2], replicated, may hold values from 0.5 to 2
- alpha_string: int32 [1024], P('alpha'), may hold values from 0 to 65535
- beta_string: int32 [4096], P('beta'), may hold values from 0 to 65535
- alpha_energy: float32 [65536], replicated, may hold values from -4 to 4
- beta_energy: float32 [65536], replicated, may hold values from -4 to 4
Outputs:
- sigma: float32 [1024, 4096], P('alpha', ('beta', 'task'))
The draws below stay inside these ranges and needn't reach their ends.
Inputs may be any that keep to these rules, and one draw needn't show every extreme that they name: Every op_alpha[k] is a symmetric matrix. Every op_beta[k] is a symmetric matrix.
All inputs are finite; a program needn't handle non-finite values.
Results may differ from the reference program's by a relative error of at most 0.0001.
Values sent between devices are 32-bit elements; how exact they have to be, the bound alone decides.
A program may use at most 128 MiB of HBM per device.

```python
import math
import jax
import jax.numpy as jnp
from jax import lax

STR = 65536
NA = 1024
NB = 4096
K = 2


def symmetric_stack(key, amount, order):
    raw = jnp.clip(jax.random.normal(key, (amount, order, order), jnp.float32), -4.0, 4.0)
    return (raw + jnp.swapaxes(raw, 1, 2)) * (0.70710678 / jnp.sqrt(jnp.float32(order)))


def draw_op_alpha(key, part):
    return symmetric_stack(jax.random.fold_in(key, 11), K, NA)


def draw_op_beta(key, part):
    return symmetric_stack(jax.random.fold_in(key, 23), K, NB)


def with_ends(drawn, key, smallest, high):
    longest = drawn.shape.index(max(drawn.shape))
    spots = []
    for shift in (0, 1):
        where = [jax.random.randint(jax.random.fold_in(key, axis), (), 0, length) for axis, length in enumerate(drawn.shape)]
        where[longest] = (where[longest] + shift) % drawn.shape[longest]
        spots.append(tuple(where))
    return drawn.at[spots[0]].set(smallest).at[spots[1]].set(high)


def shard_levels(rng, shape, split, low, largest):
    def one(dim, blocks):
        steps = jax.random.uniform(jax.random.fold_in(jax.random.fold_in(rng, 6), dim), (blocks,), jnp.float32, low / len(split), largest / len(split))
        return jnp.repeat(jnp.exp(steps), shape[dim] // blocks).reshape((-1,) + (1,) * (len(shape) - dim - 1))

    gain = one(*split[0])
    for cut in split[1:]:
        gain = gain * one(*cut)
    return gain


def bell_draw(key, extent, scale, most, shards=(), dtype=jnp.bfloat16):
    result = scale * jax.random.normal(key, extent, jnp.float32)
    if shards:
        result = result * shard_levels(key, extent, shards, -0.22, 0.18)
    return jnp.clip(result, -most, most).astype(dtype)


def setup_inputs(seed: int = 0) -> dict:
    arg_keys = jax.random.split(jax.random.key(seed), 9)
    return {
        "vector": bell_draw(arg_keys[0], (NA, NB), 1.0, 6.0, ((0, 4), (1, 4)), jnp.float32),
        "op_alpha": draw_op_alpha(jax.random.fold_in(arg_keys[8], 71), 0),
        "op_beta": draw_op_beta(jax.random.fold_in(arg_keys[8], 71), 0),
        "op_weight": jnp.clip(jnp.exp(jax.random.uniform(arg_keys[3], (K,), jnp.float32, math.log(0.5), math.log(2.0))), 0.5, 2.0),
        "alpha_string": with_ends(jax.random.randint(arg_keys[4], (NA,), 0, STR), jax.random.fold_in(arg_keys[4], 1), 0, STR - 1).astype(jnp.int32),
        "beta_string": with_ends(jax.random.randint(arg_keys[5], (NB,), 0, STR), jax.random.fold_in(arg_keys[5], 1), 0, STR - 1).astype(jnp.int32),
        "alpha_energy": bell_draw(arg_keys[6], (STR,), 1.0, 4.0, (), jnp.float32),
        "beta_energy": bell_draw(arg_keys[7], (STR,), 1.0, 4.0, (), jnp.float32),
    }


def apply_operator(alpha_matrix, beta_matrix, block):
    highest = lax.Precision.HIGHEST
    left_part = jnp.dot(alpha_matrix, block, precision=highest, preferred_element_type=jnp.float32)
    right_part = jnp.dot(block, beta_matrix.T, precision=highest, preferred_element_type=jnp.float32)
    return left_part + right_part


def reference(vector, op_alpha, op_beta, op_weight, alpha_string, beta_string, alpha_energy, beta_energy):
    running = jnp.zeros(vector.shape, jnp.float32)
    for operator in range(K):
        inter = apply_operator(op_alpha[operator], op_beta[operator], vector)
        second = apply_operator(op_alpha[operator], op_beta[operator], inter)
        running = running + op_weight[operator] * second
    diag = alpha_energy[alpha_string][:, None] + beta_energy[beta_string][None, :]
    return diag * vector + 0.5 * running
```

```python
import functools

import jax
import jax.numpy as jnp
from jax import lax
from jax.experimental import pallas as pl
from jax.experimental.pallas import tpu as pltpu
from jax.sharding import PartitionSpec as P

MESH = pl.DeviceIdType.MESH
F32 = jnp.float32
BF16 = jnp.bfloat16
TILE = 256
STRIP = 128
VMEM_BUDGET = 56 * 1024 * 1024


TURNED = (((1,), (1,)), ((), ()))


def pieces_of(half):
    return [(0, half // 2), (half // 2, half // 4), (half // 2 + half // 4, half // 4)]


def block_span(i, size):
    return pl.ds(pl.multiple_of(i * size, 128), size)


def halves(x):
    high = x.astype(BF16)
    return high, (x - high.astype(F32)).astype(BF16)


def product(stack, right_high, right_low):
    rows = stack.shape[0] // 2
    both = jnp.dot(stack, right_high, preferred_element_type=F32)
    cross = jnp.dot(stack[:rows], right_low, preferred_element_type=F32)
    return both[:rows] + (both[rows:] + cross)


def look_up(table, index):
    turned = table.T
    high, rest = halves(turned)
    middle = rest
    low = (turned - high.astype(F32) - middle.astype(F32)).astype(BF16)
    shape = (table.shape[0], index.shape[1])
    hot = jnp.where(lax.broadcasted_iota(jnp.int32, shape, 0) == index // 128, 1.0, 0.0).astype(BF16)
    found = jnp.dot(high, hot, preferred_element_type=F32) + (
        jnp.dot(middle, hot, preferred_element_type=F32) + jnp.dot(low, hot, preferred_element_type=F32)
    )
    lane = lax.broadcasted_iota(jnp.int32, found.shape, 0) == lax.rem(index, 128)
    return jnp.sum(jnp.where(lane, found, 0.0), axis=0, keepdims=True)


def kernel(
    na, nb, weight_ref, v_ref, a_ref, alpha_table, beta_table, alpha_index, beta_index, b_hbm, out_ref,
    strip, b_high, b_low, v_all, v_col, a_other, a_stack, stack, total, acc, p_own, ret_out, ret_in, u_all,
    gram, gram_end, sum_out, sum_in, last_out, last_in, square, square_stack, from_task, to_task,
    alpha_part, beta_part,
    strip_sem, z_send, z_recv, r_send, a_send, a_recv, p_send, p_recv,
    e_send, e_recv, s_send, s_recv, v_send, v_recv, k_send, k_recv, u_send, u_recv, m_send, m_recv, f_send, f_recv,
):
    a = lax.axis_index("alpha")
    b = lax.axis_index("beta")
    t = lax.axis_index("task")
    rows, cols = v_ref.shape
    full_a = a_ref.shape[1]
    half = cols // 2
    slab = cols // 4
    quarter = full_a // nb
    eighth = quarter // 2
    across = lax.rem(b + 2, 4)
    core = lax.rem(b, 2)
    sibling = b + 1 - 2 * core
    diagonal = lax.rem(sibling + 2, 4)
    other = 1 - t
    coef = 0.5 * weight_ref[t]
    coef_other = 0.5 * weight_ref[other]
    inner = lax.rem(a + 1, 4) >= 2
    outer = lax.rem(a + 1, 4) < 2
    pieces = pieces_of(half)
    steps = range(len(pieces))

    def peer(d):
        return (a, a + 1 - 2 * lax.rem(a, 2), lax.rem(a + 2, 4), 3 - a)[d]

    def span(start, size):
        return pl.ds(pl.multiple_of(start, 128), size)

    def remote(src, dst, send, recv, where):
        return pltpu.make_async_remote_copy(
            src_ref=src, dst_ref=dst, send_sem=send, recv_sem=recv, device_id=where, device_id_type=MESH
        )

    def rows_of(i):
        return pl.ds(pl.multiple_of(i * rows, 8), rows)

    def local(q):
        return pl.ds(*pieces[q])

    def piece(side, q):
        return span(side * half + pieces[q][0], pieces[q][1])

    def z_copy(q, d):
        return remote(
            v_ref.at[:, piece(t, q)], v_col.at[rows_of(a), local(q)],
            z_send.at[q, d - 1], z_recv.at[q, d - 1], {"alpha": peer(d)},
        )

    def z_relay(q, d):
        ref = v_col.at[rows_of(peer(d)), local(q)]
        return remote(ref, ref, r_send.at[q, d - 2], z_recv.at[q, 4 - d], {"alpha": peer(1)})

    def a_copy():
        at = pl.ds(pl.multiple_of(core * (rows // 2), 8), rows // 2)
        return remote(a_ref.at[at, :], a_other.at[at, :], a_send.at[0], a_recv.at[0], {"task": other})

    def a_relay():
        at = pl.ds(pl.multiple_of(core * (rows // 2), 8), rows // 2)
        return remote(a_other.at[at, :], a_other.at[at, :], a_send.at[1], a_recv.at[1], {"beta": sibling})

    def slab_of(n):
        return (2 + t, 0, 1, 2 + other)[n]

    def v_copy(n):
        at = span(slab_of(n) * slab, slab)
        return remote(v_ref.at[:, at], v_all.at[b, :, at], v_send.at[n], v_recv.at[n], {"beta": across})

    def v_pass():
        ref = v_all.at[across, :, span((2 + t) * slab, slab)]
        return remote(ref, ref, v_send.at[3], v_recv.at[3], {"task": other})

    def v_near():
        return remote(v_ref, v_all.at[b], k_send.at[4], k_recv.at[4], {"beta": sibling})

    def v_relay(n):
        ref = v_all.at[across, :, span(slab_of(n) * slab, slab)]
        return remote(ref, ref, k_send.at[n], k_recv.at[n], {"beta": sibling})

    def v_relayed(n):
        ref = v_all.at[diagonal, :, span(slab_of(n) * slab, slab)]
        return remote(ref, ref, k_send.at[n], k_recv.at[n], {"beta": sibling})

    def p_copy(q):
        at = local(q)
        return remote(ret_out.at[:, at], ret_in.at[:, at], p_send.at[q], p_recv.at[q], {"task": other})

    def u_copy(n, k, side, q):
        block = across if n == 2 else b
        ref = u_all.at[block, :, piece(side, q)]
        where = {"beta": across} if n == 0 else {"beta": sibling}
        return remote(ref, ref, u_send.at[n, k], u_recv.at[n, k], where)

    far = span(rows * jnp.where(a == 0, 1, 0), (na - 1) * rows)
    far_pair = span(rows * jnp.where(a < 2, 2, 0), 2 * rows)

    def e_copy(n):
        if n == 0:
            return remote(gram.at[:, far], gram_end.at[:, far], e_send.at[0], e_recv.at[0], {"alpha": peer(1)})
        if n == 1:
            return remote(sum_out, sum_in, e_send.at[1], e_recv.at[1], {"alpha": peer(3)})
        return remote(last_out, last_in, e_send.at[2], e_recv.at[2], {"alpha": peer(1)})

    def s_copy():
        ref = square.at[:, span(b * quarter + t * eighth, eighth)]
        return remote(ref, ref, s_send, s_recv, {"task": other})

    def m_copy(n):
        ref = square.at[:, span((across if n == 2 else b) * quarter, quarter)]
        where = {"beta": across} if n == 0 else {"beta": sibling}
        return remote(ref, ref, m_send.at[n], m_recv.at[n], where)

    def f_copy(q):
        at = pl.ds(q * TILE, TILE)
        return remote(to_task.at[:, at], from_task.at[:, at], f_send.at[q], f_recv.at[q], {"task": other})

    strips = cols // STRIP

    def strip_copy(r, slot):
        return pltpu.make_async_copy(
            b_hbm.at[pl.ds(pl.multiple_of(r * STRIP, STRIP), STRIP), :], strip.at[slot], strip_sem.at[slot]
        )

    barrier = pltpu.get_barrier_semaphore()
    for d in range(1, na):
        pl.semaphore_signal(barrier, inc=1, device_id={"alpha": lax.rem(a + d, na)}, device_id_type=MESH)
    pl.semaphore_signal(barrier, inc=1, device_id={"task": other}, device_id_type=MESH)
    pl.semaphore_signal(barrier, inc=1, device_id={"beta": across}, device_id_type=MESH)
    pl.semaphore_signal(barrier, inc=1, device_id={"beta": sibling}, device_id_type=MESH)
    strip_copy(0, 0).start()
    strip_copy(1, 1).start()
    pl.semaphore_wait(barrier, na + 2)

    v_copy(0).start()
    a_copy().start()
    for q in steps:
        z_copy(q, 1).start()

        @pl.when(outer)
        def _():
            z_copy(q, 2).start()

        @pl.when(inner)
        def _():
            z_copy(q, 3).start()

    v_copy(1).start()
    v_copy(2).start()
    v_near().start()

    def take_strip(r, carry):
        slot = lax.rem(r, 2)
        strip_copy(r, slot).wait()
        at = pl.ds(pl.multiple_of(r * STRIP, STRIP), STRIP)

        def turn(n, inside):
            wide = span(n * 512, 512)
            b_high[at, wide], b_low[at, wide] = halves(strip[slot, :, wide])
            return inside

        lax.fori_loop(0, nb * cols // 512, turn, carry)

        @pl.when(r + 2 < strips)
        def _():
            strip_copy(r + 2, slot).start()

        return carry

    lax.fori_loop(0, strips, take_strip, 0)

    def multiply(lhs, rhs_high, rhs_low):
        n = lhs.shape[0] // 2
        both = lax.dot_general(lhs, rhs_high, TURNED, preferred_element_type=F32)
        cross = lax.dot_general(lhs[:n], rhs_low, TURNED, preferred_element_type=F32)
        return both[:n] + (both[n:] + cross)

    def accumulate(into, value, block, parts, start, size, first=False):
        for at in parts:
            stack[:rows, at], stack[rows:, at] = halves(value[:, at])

        def joined(ref, at_rows, shift):
            found = [ref[at_rows, pl.ds(pl.multiple_of(shift + at.start, 128), at.size)] for at in parts]
            return found[0] if len(found) == 1 else jnp.concatenate(found, axis=1)

        at = span(start, size)
        term = multiply(joined(stack, slice(None), 0), joined(b_high, at, block * cols), joined(b_low, at, block * cols))
        into[:, at] = term if first else into[:, at] + term

    whole = [pl.ds(0, cols)]

    def relay_z(q):
        @pl.when(inner)
        def _():
            for d in (3, 2):
                z_copy(q, d).wait_recv()
                z_relay(q, d).start()

    def project(q):
        z_copy(q, 1).wait_recv()

        @pl.when(outer)
        def _():
            for d in (2, 3):
                z_copy(q, d).wait_recv()

        both = 2.0 * product(a_stack[...], *halves(v_col[:, local(q)]))
        ret_out[:, local(q)] = both[rows:]
        p_copy(q).start()
        p_own[:, local(q)] = both[:rows]

    order = []

    def make_u(side, q):
        if side is other:
            p_copy(q).wait_recv()
        at = piece(side, q)
        u_all[b, :, at] = total[:, at] + (ret_in if side is other else p_own)[:, local(q)]
        k = len(order)
        order.append((k, side, q))
        u_copy(0, k, side, q).start()
        u_copy(1, k, side, q).start()

    def u_parts(q0, q1):
        start = pieces[q0][0]
        size = pieces[q1][0] + pieces[q1][1] - start
        return [pl.ds(start, size), pl.ds(half + start, size)]

    accumulate(total, v_ref, b, whole, 0, cols, True)
    v_copy(0).wait_recv()
    v_pass().start()
    v_relay(0).start()
    relay_z(0)
    v_near().wait_recv()
    accumulate(total, v_all.at[sibling], sibling, whole, 0, cols)
    a_copy().wait_recv()
    a_relay().start()
    v_copy(1).wait_recv()
    v_relay(1).start()
    own_high, own_low = halves(a_ref[...])
    a_stack[:rows, :] = own_high
    a_stack[2 * rows:3 * rows, :] = own_low
    v_col[rows_of(a), :] = v_ref[:, span(t * half, half)]
    beta_part[...] = look_up(beta_table[...], beta_index[:, span(t * half, half)])
    a_relay().wait_recv()
    other_high, other_low = halves(a_other[...])
    a_stack[rows:2 * rows, :] = other_high
    a_stack[3 * rows:, :] = other_low
    at = span(b * quarter + t * eighth, eighth)
    left = jnp.concatenate([(coef * a_ref[:, at]).T, (coef_other * a_other[:, at]).T], axis=1)
    left_high, left_low = halves(left)
    a_high, a_low = a_stack[:2 * rows, :], a_stack[2 * rows:, :]
    gram[...] = jnp.dot(left_high, a_high, preferred_element_type=F32) + (
        jnp.dot(left_low, a_high, preferred_element_type=F32) + jnp.dot(left_high, a_low, preferred_element_type=F32)
    )

    @pl.when(outer)
    def _():
        e_copy(0).start()

    project(0)
    relay_z(1)
    v_copy(2).wait_recv()
    v_relay(2).start()
    v_pass().wait_recv()
    v_relay(3).start()
    accumulate(total, v_all.at[across], across, whole, 0, cols)
    for n in range(4):
        v_relayed(n).wait_recv()
    accumulate(total, v_all.at[diagonal], diagonal, whole, 0, cols)

    def relay_u(k):
        u_copy(0, *order[k]).wait_recv()
        u_copy(2, *order[k]).start()

    make_u(t, 0)
    make_u(other, 0)
    relay_z(2)
    accumulate(acc, u_all.at[b], b, u_parts(0, 0), 0, cols, True)
    u_copy(1, *order[0]).wait_recv()
    u_copy(1, *order[1]).wait_recv()
    accumulate(acc, u_all.at[sibling], sibling, u_parts(0, 0), 0, cols)

    @pl.when(inner)
    def _():
        e_copy(0).wait_recv()
        sum_out[...] = gram[:, far_pair] + gram_end[:, far_pair]
        e_copy(1).start()

    project(1)
    make_u(t, 1)
    relay_u(0)
    make_u(other, 1)
    alpha_row = look_up(alpha_table[...], alpha_index[...])
    alpha_part[...] = jnp.broadcast_to(alpha_row, (128, rows)).T

    @pl.when(inner)
    def _():
        e_copy(1).wait_recv()
        last_out[...] = gram[:, block_span(peer(1), rows)] + sum_in[:, block_span(a - 1, rows)]
        e_copy(2).start()
        kept = gram[:, block_span(a, rows)] + (gram_end[:, block_span(a, rows)] + sum_in[:, block_span(2 - a, rows)])
        square[:, span(b * quarter + t * eighth, eighth)] = kept.T

    relay_u(1)
    accumulate(acc, u_all.at[across], across, u_parts(0, 0), 0, cols)
    project(2)
    make_u(t, 2)
    u_copy(2, *order[0]).wait_recv()
    u_copy(2, *order[1]).wait_recv()
    accumulate(acc, u_all.at[diagonal], diagonal, u_parts(0, 0), 0, cols)
    relay_u(2)
    make_u(other, 2)

    @pl.when(outer)
    def _():
        e_copy(2).wait_recv()
        square[:, span(b * quarter + t * eighth, eighth)] = (gram[:, block_span(a, rows)] + last_in[...]).T

    s_copy().start()
    relay_u(3)
    accumulate(acc, u_all.at[b], b, u_parts(1, 2), 0, cols)
    for k in range(2, len(order)):
        u_copy(1, *order[k]).wait_recv()
    accumulate(acc, u_all.at[sibling], sibling, u_parts(1, 2), 0, cols)
    relay_u(4)
    s_copy().wait_recv()
    m_copy(0).start()
    m_copy(1).start()
    relay_u(5)
    accumulate(acc, u_all.at[across], across, u_parts(1, 2), other * half, half)
    for k in range(2, len(order)):
        u_copy(2, *order[k]).wait_recv()
    for q in range(half // TILE):
        at = span(other * half + q * TILE, TILE)
        accumulate(acc, u_all.at[diagonal], diagonal, u_parts(1, 2), other * half + q * TILE, TILE)
        to_task[:, q * TILE:(q + 1) * TILE] = coef * acc[:, at]
        f_copy(q).start()
    accumulate(acc, u_all.at[across], across, u_parts(1, 2), t * half, half)
    accumulate(acc, u_all.at[diagonal], diagonal, u_parts(1, 2), t * half, half)
    m_copy(0).wait_recv()
    m_copy(2).start()
    m_copy(1).wait_recv()
    m_copy(2).wait_recv()
    square_stack[:rows, :], square_stack[rows:, :] = halves(square[...])
    for q in range(half // TILE):
        at = span(t * half + q * TILE, TILE)
        within = pl.ds(q * TILE, TILE)
        diag = alpha_part[:, :1] + beta_part[:, within]
        acc[:, at] = coef * acc[:, at] + product(square_stack[...], *halves(v_col[:, within])) + diag * v_ref[:, at]
    for q in range(half // TILE):
        f_copy(q).wait_recv()
        within = pl.ds(q * TILE, TILE)
        out_ref[:, within] = acc[:, span(t * half + q * TILE, TILE)] + from_task[:, within]

    for q in range(half // TILE):
        f_copy(q).wait_send()
    for q in steps:
        z_copy(q, 1).wait_send()
        p_copy(q).wait_send()

        @pl.when(outer)
        def _():
            z_copy(q, 2).wait_send()

        @pl.when(inner)
        def _():
            z_copy(q, 3).wait_send()
            z_relay(q, 2).wait_send()
            z_relay(q, 3).wait_send()

    @pl.when(outer)
    def _():
        e_copy(0).wait_send()

    @pl.when(inner)
    def _():
        e_copy(1).wait_send()
        e_copy(2).wait_send()

    a_copy().wait_send()
    a_relay().wait_send()
    for n in range(3):
        v_copy(n).wait_send()
        m_copy(n).wait_send()
        for piece_of in order:
            u_copy(n, *piece_of).wait_send()
    v_pass().wait_send()
    v_near().wait_send()
    for n in range(4):
        v_relay(n).wait_send()
    s_copy().wait_send()


def scratch(na, nb, rows, cols, full_a):
    quarter = full_a // nb
    eighth = quarter // 2
    half = cols // 2
    buffers = [
        pltpu.VMEM((2, STRIP, nb * cols), F32),
        pltpu.VMEM((cols, nb * cols), BF16),
        pltpu.VMEM((cols, nb * cols), BF16),
        pltpu.VMEM((nb, rows, cols), F32),
        pltpu.VMEM((full_a, half), F32),
        pltpu.VMEM((rows, full_a), F32),
        pltpu.VMEM((4 * rows, full_a), BF16),
        pltpu.VMEM((2 * rows, cols), BF16),
        pltpu.VMEM((rows, cols), F32),
        pltpu.VMEM((rows, cols), F32),
        pltpu.VMEM((rows, half), F32),
        pltpu.VMEM((rows, half), F32),
        pltpu.VMEM((rows, half), F32),
        pltpu.VMEM((nb, rows, cols), F32),
        pltpu.VMEM((eighth, full_a), F32),
        pltpu.VMEM((eighth, full_a), F32),
        pltpu.VMEM((eighth, 2 * rows), F32),
        pltpu.VMEM((eighth, 2 * rows), F32),
        pltpu.VMEM((eighth, rows), F32),
        pltpu.VMEM((eighth, rows), F32),
        pltpu.VMEM((rows, full_a), F32),
        pltpu.VMEM((2 * rows, full_a), BF16),
        pltpu.VMEM((rows, half), F32),
        pltpu.VMEM((rows, half), F32),
        pltpu.VMEM((rows, 128), F32),
        pltpu.VMEM((1, half), F32),
    ]
    dma = pltpu.SemaphoreType.DMA
    tiles = half // TILE
    parts = len(pieces_of(half))
    counts = [
        (2,), (parts, 3), (parts, 3), (parts, 2), (2,), (2,), (parts,), (parts,),
        (3,), (3,), (), (), (4,), (4,), (5,), (5,), (3, 2 * parts), (3, 2 * parts), (3,), (3,), (tiles,), (tiles,),
    ]
    return buffers, [dma(c) if c else dma for c in counts]


def fused(
    mesh, op_weight, vector, alpha_rows, beta_rows, alpha_string, beta_string, alpha_energy, beta_energy
):
    na, nb = mesh.shape["alpha"], mesh.shape["beta"]
    rows, cols = vector.shape
    buffers, semaphores = scratch(na, nb, rows, cols, alpha_rows.shape[1])
    vmem = pl.BlockSpec(memory_space=pltpu.VMEM)
    return pl.pallas_call(
        functools.partial(kernel, na, nb),
        out_shape=jax.ShapeDtypeStruct((rows, cols // 2), F32),
        in_specs=[pl.BlockSpec(memory_space=pltpu.SMEM)] + [vmem] * 6 + [pl.BlockSpec(memory_space=pl.ANY)],
        out_specs=vmem,
        scratch_shapes=buffers + semaphores,
        compiler_params=pltpu.CompilerParams(
            collective_id=0, has_side_effects=True, vmem_limit_bytes=60 * 1024 * 1024
        ),
    )(
        op_weight, vector, alpha_rows, alpha_energy.reshape(-1, 128), beta_energy.reshape(-1, 128),
        alpha_string.reshape(1, -1), beta_string.reshape(1, -1), beta_rows,
    )


def fits(mesh, vector, alpha_rows, alpha_energy, beta_energy):
    na, nb, nt = mesh.shape["alpha"], mesh.shape["beta"], mesh.shape["task"]
    rows, cols = vector.shape
    full_a = alpha_rows.shape[1]
    if nb != 4 or nt != 2 or na != 4 or cols % (8 * 128) or rows % 128 or full_a % (256 * nb) or full_a != na * rows:
        return False
    if alpha_energy.size % 128 or beta_energy.size % 128:
        return False
    buffers, _ = scratch(na, nb, rows, cols, full_a)
    size = sum(buf.dtype.itemsize * functools.reduce(lambda x, y: x * y, buf.shape) for buf in buffers)
    size += 4 * (rows * cols + rows * full_a + rows * cols // 2)
    return size < VMEM_BUDGET


def collective(coefficient, vector, alpha_rows, beta_rows):
    high = lax.Precision.HIGH

    def dot(x, y):
        return jnp.dot(x, y, precision=high, preferred_element_type=F32)

    def apply_operator(block):
        left = dot(alpha_rows, lax.all_gather(block, "alpha", axis=0, tiled=True))
        return left + lax.psum_scatter(dot(block, beta_rows), "beta", scatter_dimension=1, tiled=True)

    second = apply_operator(apply_operator(vector))
    return lax.psum_scatter(coefficient * second, "task", scatter_dimension=1, tiled=True)


def on_device(
    mesh, vector, op_alpha, op_beta, op_weight, alpha_string, beta_string, alpha_energy, beta_energy
):
    if fits(mesh, vector, op_alpha[0], alpha_energy, beta_energy):
        return fused(
            mesh, op_weight, vector, op_alpha[0], op_beta[0],
            alpha_string, beta_string, alpha_energy, beta_energy,
        )
    task_index = lax.axis_index("task")
    summed = collective(0.5 * op_weight[task_index], vector, op_alpha[0], op_beta[0])
    width = summed.shape[1]
    column_start = task_index * width
    own_strings = lax.dynamic_slice_in_dim(beta_string, column_start, width, 0)
    own_vector = lax.dynamic_slice_in_dim(vector, column_start, width, 1)
    diag = alpha_energy[alpha_string][:, None] + beta_energy[own_strings][None, :]
    return summed + diag * own_vector


def solution(mesh):
    return jax.shard_map(
        functools.partial(on_device, mesh),
        mesh=mesh,
        in_specs=(
            P("alpha", "beta"),
            P("task", "alpha", None),
            P("task", "beta", None),
            P(),
            P("alpha"),
            P("beta"),
            P(),
            P(),
        ),
        out_specs=P("alpha", ("beta", "task")),
        check_vma=False,
    )
```

```python
import functools

import jax
import jax.numpy as jnp
from jax import lax
from jax.experimental import pallas as pl
from jax.experimental.pallas import tpu as pltpu
from jax.sharding import PartitionSpec as P

MESH = pl.DeviceIdType.MESH
F32 = jnp.float32
BF16 = jnp.bfloat16
TILE = 256
STRIP = 128
VMEM_BUDGET = 56 * 1024 * 1024


TURNED = (((1,), (1,)), ((), ()))


def pieces_of(half):
    return [(n * (half // 4), half // 4) for n in range(4)]


def block_span(i, size):
    return pl.ds(pl.multiple_of(i * size, 128), size)


def halves(x):
    high = x.astype(BF16)
    return high, (x - high.astype(F32)).astype(BF16)


def product(stack, right_high, right_low):
    rows = stack.shape[0] // 2
    both = jnp.dot(stack, right_high, preferred_element_type=F32)
    cross = jnp.dot(stack[:rows], right_low, preferred_element_type=F32)
    return both[:rows] + (both[rows:] + cross)


def look_up(table, index):
    turned = table.T
    high, rest = halves(turned)
    middle = rest
    low = (turned - high.astype(F32) - middle.astype(F32)).astype(BF16)
    shape = (table.shape[0], index.shape[1])
    hot = jnp.where(lax.broadcasted_iota(jnp.int32, shape, 0) == index // 128, 1.0, 0.0).astype(BF16)
    found = jnp.dot(high, hot, preferred_element_type=F32) + (
        jnp.dot(middle, hot, preferred_element_type=F32) + jnp.dot(low, hot, preferred_element_type=F32)
    )
    lane = lax.broadcasted_iota(jnp.int32, found.shape, 0) == lax.rem(index, 128)
    return jnp.sum(jnp.where(lane, found, 0.0), axis=0, keepdims=True)


def kernel(
    na, nb, weight_ref, v_hbm, a_hbm, alpha_hbm, beta_hbm, alpha_index, beta_index, b_hbm, out_ref,
    a_ref, alpha_table, beta_table, strip, b_high, b_low, v_all, v_col, a_other, a_stack, stack, total, acc, p_own, ret_out, ret_in, u_all,
    gram, gram_end, sum_out, sum_in, last_out, last_in, square, square_stack, from_task, to_task,
    alpha_part, beta_part,
    local_sem, strip_sem, z_send, z_recv, r_send, a_send, a_recv, p_send, p_recv,
    e_send, e_recv, s_send, s_recv, v_send, v_recv, k_send, k_recv, u_send, u_recv, m_send, m_recv, f_send, f_recv,
):
    a = lax.axis_index("alpha")
    b = lax.axis_index("beta")
    t = lax.axis_index("task")
    rows, cols = v_hbm.shape
    full_a = a_hbm.shape[1]
    half = cols // 2
    slab = cols // 4
    quarter = full_a // nb
    eighth = quarter // 2
    across = lax.rem(b + 2, 4)
    core = lax.rem(b, 2)
    sibling = b + 1 - 2 * core
    diagonal = lax.rem(sibling + 2, 4)
    other = 1 - t
    coef = 0.5 * weight_ref[t]
    coef_other = 0.5 * weight_ref[other]
    inner = lax.rem(a + 1, 4) >= 2
    outer = lax.rem(a + 1, 4) < 2
    pieces = pieces_of(half)
    steps = range(len(pieces))

    def peer(d):
        return (a, a + 1 - 2 * lax.rem(a, 2), lax.rem(a + 2, 4), 3 - a)[d]

    def span(start, size):
        return pl.ds(pl.multiple_of(start, 128), size)

    def remote(src, dst, send, recv, where):
        return pltpu.make_async_remote_copy(
            src_ref=src, dst_ref=dst, send_sem=send, recv_sem=recv, device_id=where, device_id_type=MESH
        )

    def rows_of(i):
        return pl.ds(pl.multiple_of(i * rows, 8), rows)

    def local(q):
        return pl.ds(*pieces[q])

    def piece(side, q):
        return span(side * half + pieces[q][0], pieces[q][1])

    def z_copy(q, d):
        return remote(
            v_hbm.at[:, piece(t, q)], v_col.at[rows_of(a), local(q)],
            z_send.at[q, d - 1], z_recv.at[q, d - 1], {"alpha": peer(d)},
        )

    def z_relay(q, d):
        ref = v_col.at[rows_of(peer(d)), local(q)]
        return remote(ref, ref, r_send.at[q, d - 2], z_recv.at[q, 4 - d], {"alpha": peer(1)})

    def a_copy():
        at = pl.ds(pl.multiple_of(core * (rows // 2), 8), rows // 2)
        return remote(a_hbm.at[at, :], a_other.at[at, :], a_send.at[0], a_recv.at[0], {"task": other})

    def a_relay():
        at = pl.ds(pl.multiple_of(core * (rows // 2), 8), rows // 2)
        return remote(a_other.at[at, :], a_other.at[at, :], a_send.at[1], a_recv.at[1], {"beta": sibling})

    def slab_of(n):
        return (2 + t, 0, 1, 2 + other)[n]

    def slab_span(n):
        return span(slab_of(n) * slab, slab)

    def v_copy(n):
        at = span(slab_of(n) * slab, slab)
        return remote(v_hbm.at[:, at], v_all.at[b, :, at], v_send.at[n], v_recv.at[n], {"beta": across})

    def v_pass():
        ref = v_all.at[across, :, span((2 + t) * slab, slab)]
        return remote(ref, ref, v_send.at[3], v_recv.at[3], {"task": other})

    def v_near():
        return remote(v_hbm, v_all.at[b], k_send.at[4], k_recv.at[4], {"beta": sibling})

    def v_relay(n):
        ref = v_all.at[across, :, span(slab_of(n) * slab, slab)]
        return remote(ref, ref, k_send.at[n], k_recv.at[n], {"beta": sibling})

    def v_relayed(n):
        ref = v_all.at[diagonal, :, span(slab_of(n) * slab, slab)]
        return remote(ref, ref, k_send.at[n], k_recv.at[n], {"beta": sibling})

    def p_copy(q):
        at = local(q)
        return remote(ret_out.at[:, at], ret_in.at[:, at], p_send.at[q], p_recv.at[q], {"task": other})

    def u_copy(n, k, side, q):
        block = across if n == 2 else b
        ref = u_all.at[block, :, piece(side, q)]
        where = {"beta": across} if n == 0 else {"beta": sibling}
        return remote(ref, ref, u_send.at[n, k], u_recv.at[n, k], where)

    far = span(rows * jnp.where(a == 0, 1, 0), (na - 1) * rows)
    far_pair = span(rows * jnp.where(a < 2, 2, 0), 2 * rows)

    def e_copy(n):
        if n == 0:
            return remote(gram.at[:, far], gram_end.at[:, far], e_send.at[0], e_recv.at[0], {"alpha": peer(1)})
        if n == 1:
            return remote(sum_out, sum_in, e_send.at[1], e_recv.at[1], {"alpha": peer(3)})
        return remote(last_out, last_in, e_send.at[2], e_recv.at[2], {"alpha": peer(1)})

    def s_copy():
        ref = square.at[:, span(b * quarter + t * eighth, eighth)]
        return remote(ref, ref, s_send, s_recv, {"task": other})

    def m_copy(n):
        ref = square.at[:, span((across if n == 2 else b) * quarter, quarter)]
        where = {"beta": across} if n == 0 else {"beta": sibling}
        return remote(ref, ref, m_send.at[n], m_recv.at[n], where)

    def f_copy(q):
        at = pl.ds(q * TILE, TILE)
        return remote(to_task.at[:, at], from_task.at[:, at], f_send.at[q], f_recv.at[q], {"task": other})

    strips = cols // STRIP

    def strip_copy(r, slot):
        return pltpu.make_async_copy(
            b_hbm.at[pl.ds(pl.multiple_of(r * STRIP, STRIP), STRIP), :], strip.at[slot], strip_sem.at[slot]
        )

    def stage(n):
        source = (v_hbm, a_hbm, beta_hbm, alpha_hbm)[n]
        return pltpu.make_async_copy(source, (v_all.at[b], a_ref, beta_table, alpha_table)[n], local_sem.at[n])

    barrier = pltpu.get_barrier_semaphore()
    for d in range(1, na):
        pl.semaphore_signal(barrier, inc=1, device_id={"alpha": lax.rem(a + d, na)}, device_id_type=MESH)
    pl.semaphore_signal(barrier, inc=1, device_id={"task": other}, device_id_type=MESH)
    pl.semaphore_signal(barrier, inc=1, device_id={"beta": across}, device_id_type=MESH)
    pl.semaphore_signal(barrier, inc=1, device_id={"beta": sibling}, device_id_type=MESH)
    strip_copy(0, 0).start()
    strip_copy(1, 1).start()
    for n in range(4):
        stage(n).start()
    pl.semaphore_wait(barrier, na + 2)

    v_copy(0).start()
    a_copy().start()

    @pl.when(outer)
    def _():
        for q in steps:
            z_copy(q, 2).start()
            z_copy(q, 1).start()

    @pl.when(inner)
    def _():
        for q in steps:
            z_copy(q, 3).start()
            z_copy(q, 1).start()

    v_copy(1).start()
    v_copy(2).start()
    v_near().start()

    def take_strip(r, carry):
        slot = lax.rem(r, 2)
        strip_copy(r, slot).wait()
        at = pl.ds(pl.multiple_of(r * STRIP, STRIP), STRIP)

        def turn(n, inside):
            wide = span(n * 512, 512)
            b_high[at, wide], b_low[at, wide] = halves(strip[slot, :, wide])
            return inside

        lax.fori_loop(0, nb * cols // 512, turn, carry)

        @pl.when(r + 2 < strips)
        def _():
            strip_copy(r + 2, slot).start()

        return carry

    lax.fori_loop(0, strips, take_strip, 0)

    def multiply(lhs, rhs_high, rhs_low):
        n = lhs.shape[0] // 2
        both = lax.dot_general(lhs, rhs_high, TURNED, preferred_element_type=F32)
        cross = lax.dot_general(lhs[:n], rhs_low, TURNED, preferred_element_type=F32)
        return both[:n] + (both[n:] + cross)

    def accumulate(into, value, block, parts, start, size, first=False):
        for at in parts:
            stack[:rows, at], stack[rows:, at] = halves(value[:, at])

        def joined(ref, at_rows, shift):
            found = [ref[at_rows, pl.ds(pl.multiple_of(shift + at.start, 128), at.size)] for at in parts]
            return found[0] if len(found) == 1 else jnp.concatenate(found, axis=1)

        at = span(start, size)
        term = multiply(joined(stack, slice(None), 0), joined(b_high, at, block * cols), joined(b_low, at, block * cols))
        into[:, at] = term if first else into[:, at] + term

    whole = [pl.ds(0, cols)]

    def relay_z(q):
        @pl.when(inner)
        def _():
            for d in (3, 2):
                z_copy(q, d).wait_recv()
                z_relay(q, d).start()

    def project(q):
        z_copy(q, 1).wait_recv()

        @pl.when(outer)
        def _():
            for d in (2, 3):
                z_copy(q, d).wait_recv()

        both = 2.0 * product(a_stack[...], *halves(v_col[:, local(q)]))
        ret_out[:, local(q)] = both[rows:]
        p_copy(q).start()
        p_own[:, local(q)] = both[:rows]

    order = []

    def make_u(side, q):
        if side is other:
            p_copy(q).wait_recv()
        at = piece(side, q)
        u_all[b, :, at] = total[:, at] + (ret_in if side is other else p_own)[:, local(q)]
        k = len(order)
        order.append((k, side, q))
        u_copy(0, k, side, q).start()
        u_copy(1, k, side, q).start()

    def u_parts(q0, q1):
        start = pieces[q0][0]
        size = pieces[q1][0] + pieces[q1][1] - start
        return [pl.ds(start, size), pl.ds(half + start, size)]

    v_copy(0).wait_recv()
    v_pass().start()
    v_relay(0).start()
    for n in range(4):
        stage(n).wait()
    accumulate(total, v_all.at[b], b, whole, 0, cols, True)
    relay_z(0)
    own_high, own_low = halves(a_ref[...])
    a_stack[:rows, :] = own_high
    a_stack[2 * rows:3 * rows, :] = own_low
    v_col[rows_of(a), :] = v_all[b, :, span(t * half, half)]
    v_near().wait_recv()
    accumulate(total, v_all.at[sibling], sibling, whole, 0, cols)
    relay_z(1)
    a_copy().wait_recv()
    a_relay().start()
    v_copy(1).wait_recv()
    v_relay(1).start()
    early = [slab_span(n) for n in (0, 1)]
    late = [slab_span(n) for n in (2, 3)]
    accumulate(total, v_all.at[across], across, early, 0, cols)
    a_relay().wait_recv()
    other_high, other_low = halves(a_other[...])
    a_stack[rows:2 * rows, :] = other_high
    a_stack[3 * rows:, :] = other_low
    for n in range(2):
        v_relayed(n).wait_recv()
    accumulate(total, v_all.at[diagonal], diagonal, early, 0, cols)
    at = span(b * quarter + t * eighth, eighth)
    left = jnp.concatenate([(coef * a_ref[:, at]).T, (coef_other * a_other[:, at]).T], axis=1)
    left_high, left_low = halves(left)
    a_high, a_low = a_stack[:2 * rows, :], a_stack[2 * rows:, :]
    gram[...] = jnp.dot(left_high, a_high, preferred_element_type=F32) + (
        jnp.dot(left_low, a_high, preferred_element_type=F32) + jnp.dot(left_high, a_low, preferred_element_type=F32)
    )

    @pl.when(outer)
    def _():
        e_copy(0).start()

    v_copy(2).wait_recv()
    v_relay(2).start()
    v_pass().wait_recv()
    v_relay(3).start()
    relay_z(2)
    project(0)
    accumulate(total, v_all.at[across], across, late, 0, cols)
    for n in range(2, 4):
        v_relayed(n).wait_recv()
    accumulate(total, v_all.at[diagonal], diagonal, late, 0, cols)

    def relay_u(k):
        u_copy(0, *order[k]).wait_recv()
        u_copy(2, *order[k]).start()

    make_u(t, 0)
    relay_z(3)
    make_u(other, 0)
    project(1)
    make_u(t, 1)
    relay_u(0)
    beta_part[...] = look_up(beta_table[...], beta_index[:, span(t * half, half)])
    relay_u(1)
    make_u(other, 1)
    accumulate(acc, u_all.at[b], b, u_parts(0, 1), 0, cols, True)
    project(2)
    make_u(t, 2)
    for k in range(4):
        u_copy(1, *order[k]).wait_recv()
    accumulate(acc, u_all.at[sibling], sibling, u_parts(0, 1), 0, cols)
    relay_u(2)

    @pl.when(inner)
    def _():
        e_copy(0).wait_recv()
        sum_out[...] = gram[:, far_pair] + gram_end[:, far_pair]
        e_copy(1).start()

    relay_u(3)
    make_u(other, 2)
    project(3)
    make_u(t, 3)
    accumulate(acc, u_all.at[across], across, u_parts(0, 1), 0, cols)
    relay_u(4)

    @pl.when(inner)
    def _():
        e_copy(1).wait_recv()
        last_out[...] = gram[:, block_span(peer(1), rows)] + sum_in[:, block_span(a - 1, rows)]
        e_copy(2).start()
        kept = gram[:, block_span(a, rows)] + (gram_end[:, block_span(a, rows)] + sum_in[:, block_span(2 - a, rows)])
        square[:, span(b * quarter + t * eighth, eighth)] = kept.T

    for k in range(4):
        u_copy(2, *order[k]).wait_recv()
    accumulate(acc, u_all.at[diagonal], diagonal, u_parts(0, 1), 0, cols)
    make_u(other, 3)
    relay_u(5)

    @pl.when(outer)
    def _():
        e_copy(2).wait_recv()
        square[:, span(b * quarter + t * eighth, eighth)] = (gram[:, block_span(a, rows)] + last_in[...]).T

    s_copy().start()
    accumulate(acc, u_all.at[b], b, u_parts(2, 3), 0, cols)
    relay_u(6)
    for k in range(4, len(order)):
        u_copy(1, *order[k]).wait_recv()
    accumulate(acc, u_all.at[sibling], sibling, u_parts(2, 3), 0, cols)
    s_copy().wait_recv()
    m_copy(0).start()
    m_copy(1).start()
    most = [piece(t, 2), piece(t, 3), piece(other, 2)]
    last = [piece(other, 3)]
    accumulate(acc, u_all.at[across], across, most, other * half, half)
    for k in range(4, len(order) - 1):
        u_copy(2, *order[k]).wait_recv()
    accumulate(acc, u_all.at[diagonal], diagonal, most, other * half, half)
    relay_u(7)
    accumulate(acc, u_all.at[across], across, last, other * half, half)
    u_copy(2, *order[7]).wait_recv()
    accumulate(acc, u_all.at[diagonal], diagonal, last, other * half, half)
    for q in range(half // TILE):
        at = span(other * half + q * TILE, TILE)
        to_task[:, q * TILE:(q + 1) * TILE] = coef * acc[:, at]
        f_copy(q).start()
    alpha_row = look_up(alpha_table[...], alpha_index[...])
    alpha_part[...] = jnp.broadcast_to(alpha_row, (128, rows)).T
    accumulate(acc, u_all.at[across], across, u_parts(2, 3), t * half, half)
    accumulate(acc, u_all.at[diagonal], diagonal, u_parts(2, 3), t * half, half)
    m_copy(0).wait_recv()
    m_copy(2).start()
    m_copy(1).wait_recv()
    m_copy(2).wait_recv()
    square_stack[:rows, :], square_stack[rows:, :] = halves(square[...])
    for q in range(half // TILE):
        at = span(t * half + q * TILE, TILE)
        within = pl.ds(q * TILE, TILE)
        diag = alpha_part[:, :1] + beta_part[:, within]
        acc[:, at] = coef * acc[:, at] + product(square_stack[...], *halves(v_col[:, within])) + diag * v_all[b, :, at]
    for q in range(half // TILE):
        f_copy(q).wait_recv()
        within = pl.ds(q * TILE, TILE)
        out_ref[:, within] = acc[:, span(t * half + q * TILE, TILE)] + from_task[:, within]

    for q in range(half // TILE):
        f_copy(q).wait_send()
    for q in steps:
        z_copy(q, 1).wait_send()
        p_copy(q).wait_send()

        @pl.when(outer)
        def _():
            z_copy(q, 2).wait_send()

        @pl.when(inner)
        def _():
            z_copy(q, 3).wait_send()
            z_relay(q, 2).wait_send()
            z_relay(q, 3).wait_send()

    @pl.when(outer)
    def _():
        e_copy(0).wait_send()

    @pl.when(inner)
    def _():
        e_copy(1).wait_send()
        e_copy(2).wait_send()

    a_copy().wait_send()
    a_relay().wait_send()
    for n in range(3):
        v_copy(n).wait_send()
        m_copy(n).wait_send()
        for piece_of in order:
            u_copy(n, *piece_of).wait_send()
    v_pass().wait_send()
    v_near().wait_send()
    for n in range(4):
        v_relay(n).wait_send()
    s_copy().wait_send()


def scratch(na, nb, rows, cols, full_a, alpha_size, beta_size):
    quarter = full_a // nb
    eighth = quarter // 2
    half = cols // 2
    buffers = [
        pltpu.VMEM((rows, full_a), F32),
        pltpu.VMEM((alpha_size // 128, 128), F32),
        pltpu.VMEM((beta_size // 128, 128), F32),
        pltpu.VMEM((2, STRIP, nb * cols), F32),
        pltpu.VMEM((cols, nb * cols), BF16),
        pltpu.VMEM((cols, nb * cols), BF16),
        pltpu.VMEM((nb, rows, cols), F32),
        pltpu.VMEM((full_a, half), F32),
        pltpu.VMEM((rows, full_a), F32),
        pltpu.VMEM((4 * rows, full_a), BF16),
        pltpu.VMEM((2 * rows, cols), BF16),
        pltpu.VMEM((rows, cols), F32),
        pltpu.VMEM((rows, cols), F32),
        pltpu.VMEM((rows, half), F32),
        pltpu.VMEM((rows, half), F32),
        pltpu.VMEM((rows, half), F32),
        pltpu.VMEM((nb, rows, cols), F32),
        pltpu.VMEM((eighth, full_a), F32),
        pltpu.VMEM((eighth, full_a), F32),
        pltpu.VMEM((eighth, 2 * rows), F32),
        pltpu.VMEM((eighth, 2 * rows), F32),
        pltpu.VMEM((eighth, rows), F32),
        pltpu.VMEM((eighth, rows), F32),
        pltpu.VMEM((rows, full_a), F32),
        pltpu.VMEM((2 * rows, full_a), BF16),
        pltpu.VMEM((rows, half), F32),
        pltpu.VMEM((rows, half), F32),
        pltpu.VMEM((rows, 128), F32),
        pltpu.VMEM((1, half), F32),
    ]
    dma = pltpu.SemaphoreType.DMA
    tiles = half // TILE
    parts = len(pieces_of(half))
    counts = [
        (4,), (2,), (parts, 3), (parts, 3), (parts, 2), (2,), (2,), (parts,), (parts,),
        (3,), (3,), (), (), (4,), (4,), (5,), (5,), (3, 2 * parts), (3, 2 * parts), (3,), (3,), (tiles,), (tiles,),
    ]
    return buffers, [dma(c) if c else dma for c in counts]


def fused(
    mesh, op_weight, vector, alpha_rows, beta_rows, alpha_string, beta_string, alpha_energy, beta_energy
):
    na, nb = mesh.shape["alpha"], mesh.shape["beta"]
    rows, cols = vector.shape
    buffers, semaphores = scratch(na, nb, rows, cols, alpha_rows.shape[1], alpha_energy.size, beta_energy.size)
    vmem = pl.BlockSpec(memory_space=pltpu.VMEM)
    whole = pl.BlockSpec(memory_space=pl.ANY)
    return pl.pallas_call(
        functools.partial(kernel, na, nb),
        out_shape=jax.ShapeDtypeStruct((rows, cols // 2), F32),
        in_specs=[pl.BlockSpec(memory_space=pltpu.SMEM)] + [whole] * 4 + [vmem] * 2 + [whole],
        out_specs=vmem,
        scratch_shapes=buffers + semaphores,
        compiler_params=pltpu.CompilerParams(
            collective_id=0, has_side_effects=True, vmem_limit_bytes=60 * 1024 * 1024
        ),
    )(
        op_weight, vector, alpha_rows, alpha_energy.reshape(-1, 128), beta_energy.reshape(-1, 128),
        alpha_string.reshape(1, -1), beta_string.reshape(1, -1), beta_rows,
    )


def fits(mesh, vector, alpha_rows, alpha_energy, beta_energy):
    na, nb, nt = mesh.shape["alpha"], mesh.shape["beta"], mesh.shape["task"]
    rows, cols = vector.shape
    full_a = alpha_rows.shape[1]
    if nb != 4 or nt != 2 or na != 4 or cols % (8 * 128) or rows % 128 or full_a % (256 * nb) or full_a != na * rows:
        return False
    if alpha_energy.size % 128 or beta_energy.size % 128:
        return False
    buffers, _ = scratch(na, nb, rows, cols, full_a, alpha_energy.size, beta_energy.size)
    size = sum(buf.dtype.itemsize * functools.reduce(lambda x, y: x * y, buf.shape) for buf in buffers)
    size += 2 * rows * cols
    return size < VMEM_BUDGET


def collective(coefficient, vector, alpha_rows, beta_rows):
    high = lax.Precision.HIGH

    def dot(x, y):
        return jnp.dot(x, y, precision=high, preferred_element_type=F32)

    def apply_operator(block):
        left = dot(alpha_rows, lax.all_gather(block, "alpha", axis=0, tiled=True))
        return left + lax.psum_scatter(dot(block, beta_rows), "beta", scatter_dimension=1, tiled=True)

    second = apply_operator(apply_operator(vector))
    return lax.psum_scatter(coefficient * second, "task", scatter_dimension=1, tiled=True)


def on_device(
    mesh, vector, op_alpha, op_beta, op_weight, alpha_string, beta_string, alpha_energy, beta_energy
):
    if fits(mesh, vector, op_alpha[0], alpha_energy, beta_energy):
        return fused(
            mesh, op_weight, vector, op_alpha[0], op_beta[0],
            alpha_string, beta_string, alpha_energy, beta_energy,
        )
    task_index = lax.axis_index("task")
    summed = collective(0.5 * op_weight[task_index], vector, op_alpha[0], op_beta[0])
    width = summed.shape[1]
    column_start = task_index * width
    own_strings = lax.dynamic_slice_in_dim(beta_string, column_start, width, 0)
    own_vector = lax.dynamic_slice_in_dim(vector, column_start, width, 1)
    diag = alpha_energy[alpha_string][:, None] + beta_energy[own_strings][None, :]
    return summed + diag * own_vector


def solution(mesh):
    return jax.shard_map(
        functools.partial(on_device, mesh),
        mesh=mesh,
        in_specs=(
            P("alpha", "beta"),
            P("task", "alpha", None),
            P("task", "beta", None),
            P(),
            P("alpha"),
            P("beta"),
            P(),
            P(),
        ),
        out_specs=P("alpha", ("beta", "task")),
        check_vma=False,
    )
```

```python
import functools

import jax
import jax.numpy as jnp
from jax import lax
from jax.experimental import pallas as pl
from jax.experimental.pallas import tpu as pltpu
from jax.sharding import PartitionSpec as P

MESH = pl.DeviceIdType.MESH
F32 = jnp.float32
BF16 = jnp.bfloat16
TILE = 256
STRIP = 128
VMEM_BUDGET = 56 * 1024 * 1024


TURNED = (((1,), (1,)), ((), ()))


def pieces_of(half):
    return [(n * (half // 4), half // 4) for n in range(4)]


def block_span(i, size):
    return pl.ds(pl.multiple_of(i * size, 128), size)


def halves(x):
    high = x.astype(BF16)
    return high, (x - high.astype(F32)).astype(BF16)


def product(stack, right_high, right_low):
    rows = stack.shape[0] // 2
    both = jnp.dot(stack, right_high, preferred_element_type=F32)
    cross = jnp.dot(stack[:rows], right_low, preferred_element_type=F32)
    return both[:rows] + (both[rows:] + cross)


def look_up(table, index):
    turned = table.T
    high, rest = halves(turned)
    middle = rest
    low = (turned - high.astype(F32) - middle.astype(F32)).astype(BF16)
    shape = (table.shape[0], index.shape[1])
    hot = jnp.where(lax.broadcasted_iota(jnp.int32, shape, 0) == index // 128, 1.0, 0.0).astype(BF16)
    found = jnp.dot(high, hot, preferred_element_type=F32) + (
        jnp.dot(middle, hot, preferred_element_type=F32) + jnp.dot(low, hot, preferred_element_type=F32)
    )
    lane = lax.broadcasted_iota(jnp.int32, found.shape, 0) == lax.rem(index, 128)
    return jnp.sum(jnp.where(lane, found, 0.0), axis=0, keepdims=True)


def kernel(
    na, nb, weight_ref, v_hbm, a_hbm, alpha_hbm, beta_hbm, alpha_index, beta_index, b_hbm, out_ref,
    a_ref, alpha_table, beta_table, strip, b_high, b_low, v_all, v_col, a_other, a_stack, stack, total, acc, p_own, ret_out, ret_in, u_all,
    gram, gram_end, sum_out, sum_in, last_out, last_in, square, square_stack, from_task, to_task,
    alpha_part, beta_part,
    local_sem, strip_sem, z_send, z_recv, r_send, a_send, a_recv, p_send, p_recv,
    e_send, e_recv, s_send, s_recv, v_send, v_recv, k_send, k_recv, u_send, u_recv, m_send, m_recv, f_send, f_recv,
):
    a = lax.axis_index("alpha")
    b = lax.axis_index("beta")
    t = lax.axis_index("task")
    rows, cols = v_hbm.shape
    full_a = a_hbm.shape[1]
    half = cols // 2
    slab = cols // 4
    quarter = full_a // nb
    eighth = quarter // 2
    across = lax.rem(b + 2, 4)
    core = lax.rem(b, 2)
    sibling = b + 1 - 2 * core
    diagonal = lax.rem(sibling + 2, 4)
    other = 1 - t
    coef = 0.5 * weight_ref[t]
    coef_other = 0.5 * weight_ref[other]
    inner = lax.rem(a + 1, 4) >= 2
    outer = lax.rem(a + 1, 4) < 2
    pieces = pieces_of(half)
    steps = range(len(pieces))

    def peer(d):
        return (a, a + 1 - 2 * lax.rem(a, 2), lax.rem(a + 2, 4), 3 - a)[d]

    def span(start, size):
        return pl.ds(pl.multiple_of(start, 128), size)

    def remote(src, dst, send, recv, where):
        return pltpu.make_async_remote_copy(
            src_ref=src, dst_ref=dst, send_sem=send, recv_sem=recv, device_id=where, device_id_type=MESH
        )

    def rows_of(i):
        return pl.ds(pl.multiple_of(i * rows, 8), rows)

    def local(q):
        return pl.ds(*pieces[q])

    def piece(side, q):
        return span(side * half + pieces[q][0], pieces[q][1])

    def z_copy(q, d):
        return remote(
            v_hbm.at[:, piece(t, q)], v_col.at[rows_of(a), local(q)],
            z_send.at[q, d - 1], z_recv.at[q, d - 1], {"alpha": peer(d)},
        )

    def z_relay(q, d):
        ref = v_col.at[rows_of(peer(d)), local(q)]
        return remote(ref, ref, r_send.at[q, d - 2], z_recv.at[q, 4 - d], {"alpha": peer(1)})

    def a_copy():
        at = pl.ds(pl.multiple_of(core * (rows // 2), 8), rows // 2)
        return remote(a_hbm.at[at, :], a_other.at[at, :], a_send.at[0], a_recv.at[0], {"task": other})

    def a_relay():
        at = pl.ds(pl.multiple_of(core * (rows // 2), 8), rows // 2)
        return remote(a_other.at[at, :], a_other.at[at, :], a_send.at[1], a_recv.at[1], {"beta": sibling})

    def slab_of(n):
        return (2 + t, 0, 1, 2 + other)[n]

    def slab_span(n):
        return span(slab_of(n) * slab, slab)

    def v_copy(n):
        at = span(slab_of(n) * slab, slab)
        return remote(v_hbm.at[:, at], v_all.at[b, :, at], v_send.at[n], v_recv.at[n], {"beta": across})

    def v_pass():
        ref = v_all.at[across, :, span((2 + t) * slab, slab)]
        return remote(ref, ref, v_send.at[3], v_recv.at[3], {"task": other})

    def v_near():
        return remote(v_hbm, v_all.at[b], k_send.at[4], k_recv.at[4], {"beta": sibling})

    def v_relay(n):
        ref = v_all.at[across, :, span(slab_of(n) * slab, slab)]
        return remote(ref, ref, k_send.at[n], k_recv.at[n], {"beta": sibling})

    def v_relayed(n):
        ref = v_all.at[diagonal, :, span(slab_of(n) * slab, slab)]
        return remote(ref, ref, k_send.at[n], k_recv.at[n], {"beta": sibling})

    def p_copy(q):
        at = local(q)
        return remote(ret_out.at[:, at], ret_in.at[:, at], p_send.at[q], p_recv.at[q], {"task": other})

    def u_copy(n, k, side, q):
        block = across if n == 2 else b
        ref = u_all.at[block, :, piece(side, q)]
        where = {"beta": across} if n == 0 else {"beta": sibling}
        return remote(ref, ref, u_send.at[n, k], u_recv.at[n, k], where)

    def block_of(n):
        return (3 - a, lax.rem(a + 2, 4), peer(1), lax.rem(a + 2, 4), 3 - a)[n]

    def gram_block(ref, i):
        return ref.at[:, block_span(i, rows)]

    def e_copy(n):
        if n < 3:
            return remote(
                gram_block(gram, block_of(n)), gram_block(gram_end, block_of(n)),
                e_send.at[n], e_recv.at[n], {"alpha": peer(1)},
            )
        if n < 5:
            return remote(sum_out.at[n - 3], sum_in.at[n - 3], e_send.at[n], e_recv.at[n], {"alpha": peer(3)})
        return remote(last_out, last_in, e_send.at[n], e_recv.at[n], {"alpha": peer(1)})

    def forward_sum(n):
        block = block_span(block_of(3 + n), rows)
        e_copy(n).wait_recv()
        sum_out[n] = gram[:, block] + gram_end[:, block]
        e_copy(3 + n).start()

    def s_copy():
        ref = square.at[:, span(b * quarter + t * eighth, eighth)]
        return remote(ref, ref, s_send, s_recv, {"task": other})

    def m_copy(n):
        ref = square.at[:, span((across if n == 2 else b) * quarter, quarter)]
        where = {"beta": across} if n == 0 else {"beta": sibling}
        return remote(ref, ref, m_send.at[n], m_recv.at[n], where)

    def f_copy(q):
        at = pl.ds(q * TILE, TILE)
        return remote(to_task.at[:, at], from_task.at[:, at], f_send.at[q], f_recv.at[q], {"task": other})

    strips = cols // STRIP

    def strip_copy(r, slot):
        return pltpu.make_async_copy(
            b_hbm.at[pl.ds(pl.multiple_of(r * STRIP, STRIP), STRIP), :], strip.at[slot], strip_sem.at[slot]
        )

    def stage(n):
        source = (v_hbm, a_hbm, beta_hbm, alpha_hbm)[n]
        return pltpu.make_async_copy(source, (v_all.at[b], a_ref, beta_table, alpha_table)[n], local_sem.at[n])

    barrier = pltpu.get_barrier_semaphore()
    for d in range(1, na):
        pl.semaphore_signal(barrier, inc=1, device_id={"alpha": lax.rem(a + d, na)}, device_id_type=MESH)
    pl.semaphore_signal(barrier, inc=1, device_id={"task": other}, device_id_type=MESH)
    pl.semaphore_signal(barrier, inc=1, device_id={"beta": across}, device_id_type=MESH)
    pl.semaphore_signal(barrier, inc=1, device_id={"beta": sibling}, device_id_type=MESH)
    strip_copy(0, 0).start()
    strip_copy(1, 1).start()
    for n in range(4):
        stage(n).start()
    pl.semaphore_wait(barrier, na + 2)

    v_copy(0).start()
    a_copy().start()

    @pl.when(outer)
    def _():
        for q in steps:
            z_copy(q, 2).start()
            z_copy(q, 1).start()

    @pl.when(inner)
    def _():
        for q in steps:
            z_copy(q, 3).start()
            z_copy(q, 1).start()

    v_copy(1).start()
    v_copy(2).start()
    v_near().start()

    def take_strip(r, carry):
        slot = lax.rem(r, 2)
        strip_copy(r, slot).wait()
        at = pl.ds(pl.multiple_of(r * STRIP, STRIP), STRIP)

        def turn(n, inside):
            wide = span(n * 512, 512)
            b_high[at, wide], b_low[at, wide] = halves(strip[slot, :, wide])
            return inside

        lax.fori_loop(0, nb * cols // 512, turn, carry)

        @pl.when(r + 2 < strips)
        def _():
            strip_copy(r + 2, slot).start()

        return carry

    lax.fori_loop(0, strips, take_strip, 0)

    def multiply(lhs, rhs_high, rhs_low):
        n = lhs.shape[0] // 2
        both = lax.dot_general(lhs, rhs_high, TURNED, preferred_element_type=F32)
        cross = lax.dot_general(lhs[:n], rhs_low, TURNED, preferred_element_type=F32)
        return both[:n] + (both[n:] + cross)

    def accumulate(into, value, block, parts, start, size, first=False):
        for at in parts:
            stack[:rows, at], stack[rows:, at] = halves(value[:, at])

        def joined(ref, at_rows, shift):
            found = [ref[at_rows, pl.ds(pl.multiple_of(shift + at.start, 128), at.size)] for at in parts]
            return found[0] if len(found) == 1 else jnp.concatenate(found, axis=1)

        at = span(start, size)
        term = multiply(joined(stack, slice(None), 0), joined(b_high, at, block * cols), joined(b_low, at, block * cols))
        into[:, at] = term if first else into[:, at] + term

    whole = [pl.ds(0, cols)]

    def relay_z(q):
        @pl.when(inner)
        def _():
            for d in (3, 2):
                z_copy(q, d).wait_recv()
                z_relay(q, d).start()

    def project(q):
        z_copy(q, 1).wait_recv()

        @pl.when(outer)
        def _():
            for d in (2, 3):
                z_copy(q, d).wait_recv()

        both = 2.0 * product(a_stack[...], *halves(v_col[:, local(q)]))
        ret_out[:, local(q)] = both[rows:]
        p_copy(q).start()
        p_own[:, local(q)] = both[:rows]

    order = []

    def make_u(side, q):
        if side is other:
            p_copy(q).wait_recv()
        at = piece(side, q)
        u_all[b, :, at] = total[:, at] + (ret_in if side is other else p_own)[:, local(q)]
        k = len(order)
        order.append((k, side, q))
        u_copy(0, k, side, q).start()
        u_copy(1, k, side, q).start()

    def u_parts(q0, q1):
        start = pieces[q0][0]
        size = pieces[q1][0] + pieces[q1][1] - start
        return [pl.ds(start, size), pl.ds(half + start, size)]

    v_copy(0).wait_recv()
    v_pass().start()
    v_relay(0).start()
    for n in range(4):
        stage(n).wait()
    accumulate(total, v_all.at[b], b, whole, 0, cols, True)
    relay_z(0)
    own_high, own_low = halves(a_ref[...])
    a_stack[:rows, :] = own_high
    a_stack[2 * rows:3 * rows, :] = own_low
    v_col[rows_of(a), :] = v_all[b, :, span(t * half, half)]
    v_near().wait_recv()
    accumulate(total, v_all.at[sibling], sibling, whole, 0, cols)
    relay_z(1)
    a_copy().wait_recv()
    a_relay().start()
    v_copy(1).wait_recv()
    v_relay(1).start()
    early = [slab_span(n) for n in (0, 1)]
    late = [slab_span(n) for n in (2, 3)]
    accumulate(total, v_all.at[across], across, early, 0, cols)
    a_relay().wait_recv()
    other_high, other_low = halves(a_other[...])
    a_stack[rows:2 * rows, :] = other_high
    a_stack[3 * rows:, :] = other_low
    for n in range(2):
        v_relayed(n).wait_recv()
    accumulate(total, v_all.at[diagonal], diagonal, early, 0, cols)
    at = span(b * quarter + t * eighth, eighth)
    left = jnp.concatenate([(coef * a_ref[:, at]).T, (coef_other * a_other[:, at]).T], axis=1)
    left_high, left_low = halves(left)
    a_high, a_low = a_stack[:2 * rows, :], a_stack[2 * rows:, :]
    gram[...] = jnp.dot(left_high, a_high, preferred_element_type=F32) + (
        jnp.dot(left_low, a_high, preferred_element_type=F32) + jnp.dot(left_high, a_low, preferred_element_type=F32)
    )

    @pl.when(outer)
    def _():
        for n in range(3):
            e_copy(n).start()

    v_copy(2).wait_recv()
    v_relay(2).start()
    v_pass().wait_recv()
    v_relay(3).start()
    relay_z(2)
    project(0)
    accumulate(total, v_all.at[across], across, late, 0, cols)
    for n in range(2, 4):
        v_relayed(n).wait_recv()
    accumulate(total, v_all.at[diagonal], diagonal, late, 0, cols)

    def relay_u(k):
        u_copy(0, *order[k]).wait_recv()
        u_copy(2, *order[k]).start()

    make_u(t, 0)
    relay_z(3)
    make_u(other, 0)
    project(1)
    make_u(t, 1)
    relay_u(0)
    beta_part[...] = look_up(beta_table[...], beta_index[:, span(t * half, half)])
    relay_u(1)
    make_u(other, 1)

    @pl.when(inner)
    def _():
        forward_sum(0)

    accumulate(acc, u_all.at[b], b, u_parts(0, 1), other * half, half, True)
    project(2)
    make_u(t, 2)
    for k in range(4):
        u_copy(1, *order[k]).wait_recv()
    accumulate(acc, u_all.at[sibling], sibling, u_parts(0, 1), other * half, half)
    relay_u(2)

    @pl.when(inner)
    def _():
        forward_sum(1)

    relay_u(3)

    @pl.when(inner)
    def _():
        e_copy(3).wait_recv()
        last_out[...] = gram[:, block_span(peer(1), rows)] + sum_in[0]
        e_copy(5).start()

    make_u(other, 2)
    project(3)
    make_u(t, 3)
    accumulate(acc, u_all.at[across], across, u_parts(0, 1), other * half, half)
    relay_u(4)

    for k in range(4):
        u_copy(2, *order[k]).wait_recv()
    accumulate(acc, u_all.at[diagonal], diagonal, u_parts(0, 1), other * half, half)
    make_u(other, 3)
    relay_u(5)
    accumulate(acc, u_all.at[b], b, u_parts(2, 3), other * half, half)

    @pl.when(inner)
    def _():
        e_copy(2).wait_recv()
        e_copy(4).wait_recv()
        own = block_span(a, rows)
        square[:, span(b * quarter + t * eighth, eighth)] = (gram[:, own] + (gram_end[:, own] + sum_in[1])).T

    @pl.when(outer)
    def _():
        e_copy(5).wait_recv()
        square[:, span(b * quarter + t * eighth, eighth)] = (gram[:, block_span(a, rows)] + last_in[...]).T

    s_copy().start()
    relay_u(6)
    for k in range(4, len(order)):
        u_copy(1, *order[k]).wait_recv()
    accumulate(acc, u_all.at[sibling], sibling, u_parts(2, 3), other * half, half)
    most = [piece(t, 2), piece(t, 3), piece(other, 2)]
    last = [piece(other, 3)]
    accumulate(acc, u_all.at[across], across, most, other * half, half)
    for k in range(4, len(order) - 1):
        u_copy(2, *order[k]).wait_recv()
    accumulate(acc, u_all.at[diagonal], diagonal, most, other * half, half)
    relay_u(7)
    accumulate(acc, u_all.at[across], across, last, other * half, half)
    u_copy(2, *order[7]).wait_recv()
    accumulate(acc, u_all.at[diagonal], diagonal, last, other * half, half)
    for q in range(half // TILE):
        at = span(other * half + q * TILE, TILE)
        to_task[:, q * TILE:(q + 1) * TILE] = coef * acc[:, at]
        f_copy(q).start()
    alpha_row = look_up(alpha_table[...], alpha_index[...])
    alpha_part[...] = jnp.broadcast_to(alpha_row, (128, rows)).T
    s_copy().wait_recv()
    m_copy(0).start()
    m_copy(1).start()
    accumulate(acc, u_all.at[b], b, whole, t * half, half, True)
    for block in (sibling, across, diagonal):
        accumulate(acc, u_all.at[block], block, whole, t * half, half)
    m_copy(0).wait_recv()
    m_copy(2).start()
    m_copy(1).wait_recv()
    m_copy(2).wait_recv()
    square_stack[:rows, :], square_stack[rows:, :] = halves(square[...])
    for q in range(half // TILE):
        at = span(t * half + q * TILE, TILE)
        within = pl.ds(q * TILE, TILE)
        diag = alpha_part[:, :1] + beta_part[:, within]
        acc[:, at] = coef * acc[:, at] + product(square_stack[...], *halves(v_col[:, within])) + diag * v_all[b, :, at]
    for q in range(half // TILE):
        f_copy(q).wait_recv()
        within = pl.ds(q * TILE, TILE)
        out_ref[:, within] = acc[:, span(t * half + q * TILE, TILE)] + from_task[:, within]

    for q in range(half // TILE):
        f_copy(q).wait_send()
    for q in steps:
        z_copy(q, 1).wait_send()
        p_copy(q).wait_send()

        @pl.when(outer)
        def _():
            z_copy(q, 2).wait_send()

        @pl.when(inner)
        def _():
            z_copy(q, 3).wait_send()
            z_relay(q, 2).wait_send()
            z_relay(q, 3).wait_send()

    @pl.when(outer)
    def _():
        for n in range(3):
            e_copy(n).wait_send()

    @pl.when(inner)
    def _():
        for n in range(3, 6):
            e_copy(n).wait_send()

    a_copy().wait_send()
    a_relay().wait_send()
    for n in range(3):
        v_copy(n).wait_send()
        m_copy(n).wait_send()
        for piece_of in order:
            u_copy(n, *piece_of).wait_send()
    v_pass().wait_send()
    v_near().wait_send()
    for n in range(4):
        v_relay(n).wait_send()
    s_copy().wait_send()


def scratch(na, nb, rows, cols, full_a, alpha_size, beta_size):
    quarter = full_a // nb
    eighth = quarter // 2
    half = cols // 2
    buffers = [
        pltpu.VMEM((rows, full_a), F32),
        pltpu.VMEM((alpha_size // 128, 128), F32),
        pltpu.VMEM((beta_size // 128, 128), F32),
        pltpu.VMEM((2, STRIP, nb * cols), F32),
        pltpu.VMEM((cols, nb * cols), BF16),
        pltpu.VMEM((cols, nb * cols), BF16),
        pltpu.VMEM((nb, rows, cols), F32),
        pltpu.VMEM((full_a, half), F32),
        pltpu.VMEM((rows, full_a), F32),
        pltpu.VMEM((4 * rows, full_a), BF16),
        pltpu.VMEM((2 * rows, cols), BF16),
        pltpu.VMEM((rows, cols), F32),
        pltpu.VMEM((rows, cols), F32),
        pltpu.VMEM((rows, half), F32),
        pltpu.VMEM((rows, half), F32),
        pltpu.VMEM((rows, half), F32),
        pltpu.VMEM((nb, rows, cols), F32),
        pltpu.VMEM((eighth, full_a), F32),
        pltpu.VMEM((eighth, full_a), F32),
        pltpu.VMEM((2, eighth, rows), F32),
        pltpu.VMEM((2, eighth, rows), F32),
        pltpu.VMEM((eighth, rows), F32),
        pltpu.VMEM((eighth, rows), F32),
        pltpu.VMEM((rows, full_a), F32),
        pltpu.VMEM((2 * rows, full_a), BF16),
        pltpu.VMEM((rows, half), F32),
        pltpu.VMEM((rows, half), F32),
        pltpu.VMEM((rows, 128), F32),
        pltpu.VMEM((1, half), F32),
    ]
    dma = pltpu.SemaphoreType.DMA
    tiles = half // TILE
    parts = len(pieces_of(half))
    counts = [
        (4,), (2,), (parts, 3), (parts, 3), (parts, 2), (2,), (2,), (parts,), (parts,),
        (6,), (6,), (), (), (4,), (4,), (5,), (5,), (3, 2 * parts), (3, 2 * parts), (3,), (3,), (tiles,), (tiles,),
    ]
    return buffers, [dma(c) if c else dma for c in counts]


def fused(
    mesh, op_weight, vector, alpha_rows, beta_rows, alpha_string, beta_string, alpha_energy, beta_energy
):
    na, nb = mesh.shape["alpha"], mesh.shape["beta"]
    rows, cols = vector.shape
    buffers, semaphores = scratch(na, nb, rows, cols, alpha_rows.shape[1], alpha_energy.size, beta_energy.size)
    vmem = pl.BlockSpec(memory_space=pltpu.VMEM)
    whole = pl.BlockSpec(memory_space=pl.ANY)
    return pl.pallas_call(
        functools.partial(kernel, na, nb),
        out_shape=jax.ShapeDtypeStruct((rows, cols // 2), F32),
        in_specs=[pl.BlockSpec(memory_space=pltpu.SMEM)] + [whole] * 4 + [vmem] * 2 + [whole],
        out_specs=vmem,
        scratch_shapes=buffers + semaphores,
        compiler_params=pltpu.CompilerParams(
            collective_id=0, has_side_effects=True, vmem_limit_bytes=60 * 1024 * 1024
        ),
    )(
        op_weight, vector, alpha_rows, alpha_energy.reshape(-1, 128), beta_energy.reshape(-1, 128),
        alpha_string.reshape(1, -1), beta_string.reshape(1, -1), beta_rows,
    )


def fits(mesh, vector, alpha_rows, alpha_energy, beta_energy):
    na, nb, nt = mesh.shape["alpha"], mesh.shape["beta"], mesh.shape["task"]
    rows, cols = vector.shape
    full_a = alpha_rows.shape[1]
    if nb != 4 or nt != 2 or na != 4 or cols % (8 * 128) or rows % 128 or full_a % (256 * nb) or full_a != na * rows:
        return False
    if alpha_energy.size % 128 or beta_energy.size % 128:
        return False
    buffers, _ = scratch(na, nb, rows, cols, full_a, alpha_energy.size, beta_energy.size)
    size = sum(buf.dtype.itemsize * functools.reduce(lambda x, y: x * y, buf.shape) for buf in buffers)
    size += 2 * rows * cols
    return size < VMEM_BUDGET


def collective(coefficient, vector, alpha_rows, beta_rows):
    high = lax.Precision.HIGH

    def dot(x, y):
        return jnp.dot(x, y, precision=high, preferred_element_type=F32)

    def apply_operator(block):
        left = dot(alpha_rows, lax.all_gather(block, "alpha", axis=0, tiled=True))
        return left + lax.psum_scatter(dot(block, beta_rows), "beta", scatter_dimension=1, tiled=True)

    second = apply_operator(apply_operator(vector))
    return lax.psum_scatter(coefficient * second, "task", scatter_dimension=1, tiled=True)


def on_device(
    mesh, vector, op_alpha, op_beta, op_weight, alpha_string, beta_string, alpha_energy, beta_energy
):
    if fits(mesh, vector, op_alpha[0], alpha_energy, beta_energy):
        return fused(
            mesh, op_weight, vector, op_alpha[0], op_beta[0],
            alpha_string, beta_string, alpha_energy, beta_energy,
        )
    task_index = lax.axis_index("task")
    summed = collective(0.5 * op_weight[task_index], vector, op_alpha[0], op_beta[0])
    width = summed.shape[1]
    column_start = task_index * width
    own_strings = lax.dynamic_slice_in_dim(beta_string, column_start, width, 0)
    own_vector = lax.dynamic_slice_in_dim(vector, column_start, width, 1)
    diag = alpha_energy[alpha_string][:, None] + beta_energy[own_strings][None, :]
    return summed + diag * own_vector


def solution(mesh):
    return jax.shard_map(
        functools.partial(on_device, mesh),
        mesh=mesh,
        in_specs=(
            P("alpha", "beta"),
            P("task", "alpha", None),
            P("task", "beta", None),
            P(),
            P("alpha"),
            P("beta"),
            P(),
            P(),
        ),
        out_specs=P("alpha", ("beta", "task")),
        check_vma=False,
    )
```

```python
import functools

import jax
import jax.numpy as jnp
from jax import lax
from jax.experimental import pallas as pl
from jax.experimental.pallas import tpu as pltpu
from jax.sharding import PartitionSpec as P

MESH = pl.DeviceIdType.MESH
F32 = jnp.float32
BF16 = jnp.bfloat16
TILE = 256
STRIP = 128
VMEM_BUDGET = 56 * 1024 * 1024


TURNED = (((1,), (1,)), ((), ()))


def pieces_of(half):
    return [(n * (half // 4), half // 4) for n in range(4)]


def block_span(i, size):
    return pl.ds(pl.multiple_of(i * size, 128), size)


def halves(x):
    high = x.astype(BF16)
    return high, (x - high.astype(F32)).astype(BF16)


def product(stack, right_high, right_low):
    rows = stack.shape[0] // 2
    both = jnp.dot(stack, right_high, preferred_element_type=F32)
    cross = jnp.dot(stack[:rows], right_low, preferred_element_type=F32)
    return both[:rows] + (both[rows:] + cross)


def look_up(table, index):
    turned = table.T
    high, rest = halves(turned)
    middle = rest
    low = (turned - high.astype(F32) - middle.astype(F32)).astype(BF16)
    shape = (table.shape[0], index.shape[1])
    hot = jnp.where(lax.broadcasted_iota(jnp.int32, shape, 0) == index // 128, 1.0, 0.0).astype(BF16)
    found = jnp.dot(high, hot, preferred_element_type=F32) + (
        jnp.dot(middle, hot, preferred_element_type=F32) + jnp.dot(low, hot, preferred_element_type=F32)
    )
    lane = lax.broadcasted_iota(jnp.int32, found.shape, 0) == lax.rem(index, 128)
    return jnp.sum(jnp.where(lane, found, 0.0), axis=0, keepdims=True)


def kernel(
    na, nb, weight_ref, v_hbm, a_hbm, alpha_hbm, beta_hbm, alpha_index, beta_index, b_hbm, own_out, from_task,
    a_ref, alpha_table, beta_table, strip, b_high, b_low, v_all, v_col, a_other, a_stack, stack, total, acc, p_own, ret_out, ret_in, u_all,
    gram, gram_end, sum_out, sum_in, last_out, last_in, square, square_stack, to_task,
    alpha_part, beta_part,
    local_sem, strip_sem, z_send, z_recv, r_send, a_send, a_recv, p_send, p_recv,
    e_send, e_recv, s_send, s_recv, v_send, v_recv, k_send, k_recv, u_send, u_recv, m_send, m_recv, f_send, f_recv,
):
    a = lax.axis_index("alpha")
    b = lax.axis_index("beta")
    t = lax.axis_index("task")
    rows, cols = v_hbm.shape
    full_a = a_hbm.shape[1]
    half = cols // 2
    slab = cols // 4
    quarter = full_a // nb
    eighth = quarter // 2
    across = lax.rem(b + 2, 4)
    core = lax.rem(b, 2)
    sibling = b + 1 - 2 * core
    diagonal = lax.rem(sibling + 2, 4)
    other = 1 - t
    coef = 0.5 * weight_ref[t]
    coef_other = 0.5 * weight_ref[other]
    inner = lax.rem(a + 1, 4) >= 2
    outer = lax.rem(a + 1, 4) < 2
    pieces = pieces_of(half)
    steps = range(len(pieces))

    def peer(d):
        return (a, a + 1 - 2 * lax.rem(a, 2), lax.rem(a + 2, 4), 3 - a)[d]

    def span(start, size):
        return pl.ds(pl.multiple_of(start, 128), size)

    def remote(src, dst, send, recv, where):
        return pltpu.make_async_remote_copy(
            src_ref=src, dst_ref=dst, send_sem=send, recv_sem=recv, device_id=where, device_id_type=MESH
        )

    def rows_of(i):
        return pl.ds(pl.multiple_of(i * rows, 8), rows)

    def local(q):
        return pl.ds(*pieces[q])

    def piece(side, q):
        return span(side * half + pieces[q][0], pieces[q][1])

    def z_copy(q, d):
        return remote(
            v_hbm.at[:, piece(t, q)], v_col.at[rows_of(a), local(q)],
            z_send.at[q, d - 1], z_recv.at[q, d - 1], {"alpha": peer(d)},
        )

    def z_relay(q, d):
        ref = v_col.at[rows_of(peer(d)), local(q)]
        return remote(ref, ref, r_send.at[q, d - 2], z_recv.at[q, 4 - d], {"alpha": peer(1)})

    def a_copy():
        at = pl.ds(pl.multiple_of(core * (rows // 2), 8), rows // 2)
        return remote(a_hbm.at[at, :], a_other.at[at, :], a_send.at[0], a_recv.at[0], {"task": other})

    def a_relay():
        at = pl.ds(pl.multiple_of(core * (rows // 2), 8), rows // 2)
        return remote(a_other.at[at, :], a_other.at[at, :], a_send.at[1], a_recv.at[1], {"beta": sibling})

    def slab_of(n):
        return (2 + t, 0, 1, 2 + other)[n]

    def slab_span(n):
        return span(slab_of(n) * slab, slab)

    def v_copy(n):
        at = span(slab_of(n) * slab, slab)
        return remote(v_hbm.at[:, at], v_all.at[b, :, at], v_send.at[n], v_recv.at[n], {"beta": across})

    def v_pass():
        ref = v_all.at[across, :, span((2 + t) * slab, slab)]
        return remote(ref, ref, v_send.at[3], v_recv.at[3], {"task": other})

    def v_near():
        return remote(v_hbm, v_all.at[b], k_send.at[4], k_recv.at[4], {"beta": sibling})

    def v_relay(n):
        ref = v_all.at[across, :, span(slab_of(n) * slab, slab)]
        return remote(ref, ref, k_send.at[n], k_recv.at[n], {"beta": sibling})

    def v_relayed(n):
        ref = v_all.at[diagonal, :, span(slab_of(n) * slab, slab)]
        return remote(ref, ref, k_send.at[n], k_recv.at[n], {"beta": sibling})

    def p_copy(q):
        at = local(q)
        return remote(ret_out.at[:, at], ret_in.at[:, at], p_send.at[q], p_recv.at[q], {"task": other})

    def u_copy(n, k, side, q):
        block = across if n == 2 else b
        ref = u_all.at[block, :, piece(side, q)]
        where = {"beta": across} if n == 0 else {"beta": sibling}
        return remote(ref, ref, u_send.at[n, k], u_recv.at[n, k], where)

    def block_of(n):
        return (3 - a, lax.rem(a + 2, 4), peer(1), lax.rem(a + 2, 4), 3 - a)[n]

    def gram_block(ref, i):
        return ref.at[:, block_span(i, rows)]

    def e_copy(n):
        if n < 3:
            return remote(
                gram_block(gram, block_of(n)), gram_block(gram_end, block_of(n)),
                e_send.at[n], e_recv.at[n], {"alpha": peer(1)},
            )
        if n < 5:
            return remote(sum_out.at[n - 3], sum_in.at[n - 3], e_send.at[n], e_recv.at[n], {"alpha": peer(3)})
        return remote(last_out, last_in, e_send.at[n], e_recv.at[n], {"alpha": peer(1)})

    def forward_sum(n):
        block = block_span(block_of(3 + n), rows)
        e_copy(n).wait_recv()
        sum_out[n] = gram[:, block] + gram_end[:, block]
        e_copy(3 + n).start()

    def s_copy():
        ref = square.at[:, span(b * quarter + t * eighth, eighth)]
        return remote(ref, ref, s_send, s_recv, {"task": other})

    def m_copy(n):
        ref = square.at[:, span((across if n == 2 else b) * quarter, quarter)]
        where = {"beta": across} if n == 0 else {"beta": sibling}
        return remote(ref, ref, m_send.at[n], m_recv.at[n], where)

    def f_copy(q):
        at = pl.ds(q * TILE, TILE)
        return remote(to_task.at[:, at], from_task.at[:, at], f_send.at[q], f_recv.at[q], {"task": other})

    def own_copy(q):
        at = span(t * half + q * TILE, TILE)
        return pltpu.make_async_copy(acc.at[:, at], own_out.at[:, pl.ds(q * TILE, TILE)], local_sem.at[q])

    strips = cols // STRIP

    def strip_copy(r, slot):
        return pltpu.make_async_copy(
            b_hbm.at[pl.ds(pl.multiple_of(r * STRIP, STRIP), STRIP), :], strip.at[slot], strip_sem.at[slot]
        )

    def stage(n):
        source = (v_hbm, a_hbm, beta_hbm, alpha_hbm)[n]
        return pltpu.make_async_copy(source, (v_all.at[b], a_ref, beta_table, alpha_table)[n], local_sem.at[n])

    barrier = pltpu.get_barrier_semaphore()
    for d in range(1, na):
        pl.semaphore_signal(barrier, inc=1, device_id={"alpha": lax.rem(a + d, na)}, device_id_type=MESH)
    pl.semaphore_signal(barrier, inc=1, device_id={"task": other}, device_id_type=MESH)
    pl.semaphore_signal(barrier, inc=1, device_id={"beta": across}, device_id_type=MESH)
    pl.semaphore_signal(barrier, inc=1, device_id={"beta": sibling}, device_id_type=MESH)
    strip_copy(0, 0).start()
    strip_copy(1, 1).start()
    for n in range(4):
        stage(n).start()
    pl.semaphore_wait(barrier, na + 2)

    v_copy(0).start()
    a_copy().start()

    @pl.when(outer)
    def _():
        for q in steps:
            z_copy(q, 2).start()
            z_copy(q, 1).start()

    @pl.when(inner)
    def _():
        for q in steps:
            z_copy(q, 3).start()
            z_copy(q, 1).start()

    v_copy(1).start()
    v_copy(2).start()
    v_near().start()

    def take_strip(r, carry):
        slot = lax.rem(r, 2)
        strip_copy(r, slot).wait()
        at = pl.ds(pl.multiple_of(r * STRIP, STRIP), STRIP)

        def turn(n, inside):
            wide = span(n * 512, 512)
            b_high[at, wide], b_low[at, wide] = halves(strip[slot, :, wide])
            return inside

        lax.fori_loop(0, nb * cols // 512, turn, carry)

        @pl.when(r + 2 < strips)
        def _():
            strip_copy(r + 2, slot).start()

        return carry

    lax.fori_loop(0, strips, take_strip, 0)

    def multiply(lhs, rhs_high, rhs_low):
        n = lhs.shape[0] // 2
        both = lax.dot_general(lhs, rhs_high, TURNED, preferred_element_type=F32)
        cross = lax.dot_general(lhs[:n], rhs_low, TURNED, preferred_element_type=F32)
        return both[:n] + (both[n:] + cross)

    def accumulate(into, value, block, parts, start, size, first=False):
        for at in parts:
            stack[:rows, at], stack[rows:, at] = halves(value[:, at])

        def joined(ref, at_rows, shift):
            found = [ref[at_rows, pl.ds(pl.multiple_of(shift + at.start, 128), at.size)] for at in parts]
            return found[0] if len(found) == 1 else jnp.concatenate(found, axis=1)

        at = span(start, size)
        term = multiply(joined(stack, slice(None), 0), joined(b_high, at, block * cols), joined(b_low, at, block * cols))
        into[:, at] = term if first else into[:, at] + term

    whole = [pl.ds(0, cols)]

    def relay_z(q):
        @pl.when(inner)
        def _():
            for d in (3, 2):
                z_copy(q, d).wait_recv()
                z_relay(q, d).start()

    def project(q):
        z_copy(q, 1).wait_recv()

        @pl.when(outer)
        def _():
            for d in (2, 3):
                z_copy(q, d).wait_recv()

        both = 2.0 * product(a_stack[...], *halves(v_col[:, local(q)]))
        ret_out[:, local(q)] = both[rows:]
        p_copy(q).start()
        p_own[:, local(q)] = both[:rows]

    order = []

    def make_u(side, q):
        if side is other:
            p_copy(q).wait_recv()
        at = piece(side, q)
        u_all[b, :, at] = total[:, at] + (ret_in if side is other else p_own)[:, local(q)]
        k = len(order)
        order.append((k, side, q))
        u_copy(0, k, side, q).start()
        u_copy(1, k, side, q).start()

    def u_parts(q0, q1):
        start = pieces[q0][0]
        size = pieces[q1][0] + pieces[q1][1] - start
        return [pl.ds(start, size), pl.ds(half + start, size)]

    v_copy(0).wait_recv()
    v_pass().start()
    v_relay(0).start()
    for n in range(4):
        stage(n).wait()
    accumulate(total, v_all.at[b], b, whole, 0, cols, True)
    relay_z(0)
    own_high, own_low = halves(a_ref[...])
    a_stack[:rows, :] = own_high
    a_stack[2 * rows:3 * rows, :] = own_low
    v_col[rows_of(a), :] = v_all[b, :, span(t * half, half)]
    v_near().wait_recv()
    accumulate(total, v_all.at[sibling], sibling, whole, 0, cols)
    relay_z(1)
    a_copy().wait_recv()
    a_relay().start()
    v_copy(1).wait_recv()
    v_relay(1).start()
    early = [slab_span(n) for n in (0, 1)]
    late = [slab_span(n) for n in (2, 3)]
    accumulate(total, v_all.at[across], across, early, 0, cols)
    a_relay().wait_recv()
    other_high, other_low = halves(a_other[...])
    a_stack[rows:2 * rows, :] = other_high
    a_stack[3 * rows:, :] = other_low
    for n in range(2):
        v_relayed(n).wait_recv()
    accumulate(total, v_all.at[diagonal], diagonal, early, 0, cols)
    at = span(b * quarter + t * eighth, eighth)
    left = jnp.concatenate([(coef * a_ref[:, at]).T, (coef_other * a_other[:, at]).T], axis=1)
    left_high, left_low = halves(left)
    a_high, a_low = a_stack[:2 * rows, :], a_stack[2 * rows:, :]
    gram[...] = jnp.dot(left_high, a_high, preferred_element_type=F32) + (
        jnp.dot(left_low, a_high, preferred_element_type=F32) + jnp.dot(left_high, a_low, preferred_element_type=F32)
    )

    @pl.when(outer)
    def _():
        for n in range(3):
            e_copy(n).start()

    v_copy(2).wait_recv()
    v_relay(2).start()
    v_pass().wait_recv()
    v_relay(3).start()
    relay_z(2)
    project(0)
    accumulate(total, v_all.at[across], across, late, 0, cols)
    for n in range(2, 4):
        v_relayed(n).wait_recv()
    accumulate(total, v_all.at[diagonal], diagonal, late, 0, cols)

    def relay_u(k):
        u_copy(0, *order[k]).wait_recv()
        u_copy(2, *order[k]).start()

    make_u(t, 0)
    relay_z(3)
    make_u(other, 0)
    project(1)
    make_u(t, 1)
    relay_u(0)
    beta_part[...] = look_up(beta_table[...], beta_index[:, span(t * half, half)])
    relay_u(1)
    make_u(other, 1)

    @pl.when(inner)
    def _():
        forward_sum(0)

    accumulate(acc, u_all.at[b], b, u_parts(0, 1), other * half, half, True)
    project(2)
    make_u(t, 2)
    for k in range(4):
        u_copy(1, *order[k]).wait_recv()
    accumulate(acc, u_all.at[sibling], sibling, u_parts(0, 1), other * half, half)
    relay_u(2)

    @pl.when(inner)
    def _():
        forward_sum(1)

    relay_u(3)

    @pl.when(inner)
    def _():
        e_copy(3).wait_recv()
        last_out[...] = gram[:, block_span(peer(1), rows)] + sum_in[0]
        e_copy(5).start()

    make_u(other, 2)
    project(3)
    make_u(t, 3)
    accumulate(acc, u_all.at[across], across, u_parts(0, 1), other * half, half)
    relay_u(4)

    for k in range(4):
        u_copy(2, *order[k]).wait_recv()
    accumulate(acc, u_all.at[diagonal], diagonal, u_parts(0, 1), other * half, half)
    make_u(other, 3)
    relay_u(5)
    accumulate(acc, u_all.at[b], b, u_parts(2, 3), other * half, half)

    @pl.when(inner)
    def _():
        e_copy(2).wait_recv()
        e_copy(4).wait_recv()
        own = block_span(a, rows)
        square[:, span(b * quarter + t * eighth, eighth)] = (gram[:, own] + (gram_end[:, own] + sum_in[1])).T

    @pl.when(outer)
    def _():
        e_copy(5).wait_recv()
        square[:, span(b * quarter + t * eighth, eighth)] = (gram[:, block_span(a, rows)] + last_in[...]).T

    s_copy().start()
    relay_u(6)
    for k in range(4, len(order)):
        u_copy(1, *order[k]).wait_recv()
    accumulate(acc, u_all.at[sibling], sibling, u_parts(2, 3), other * half, half)
    most = [piece(t, 2), piece(t, 3), piece(other, 2)]
    last = [piece(other, 3)]
    accumulate(acc, u_all.at[across], across, most, other * half, half)
    for k in range(4, len(order) - 1):
        u_copy(2, *order[k]).wait_recv()
    accumulate(acc, u_all.at[diagonal], diagonal, most, other * half, half)
    relay_u(7)
    accumulate(acc, u_all.at[across], across, last, other * half, half)
    u_copy(2, *order[7]).wait_recv()
    accumulate(acc, u_all.at[diagonal], diagonal, last, other * half, half)
    for q in range(half // TILE):
        at = span(other * half + q * TILE, TILE)
        to_task[:, q * TILE:(q + 1) * TILE] = coef * acc[:, at]
        f_copy(q).start()
    alpha_row = look_up(alpha_table[...], alpha_index[...])
    alpha_part[...] = jnp.broadcast_to(alpha_row, (128, rows)).T
    s_copy().wait_recv()
    m_copy(0).start()
    m_copy(1).start()
    accumulate(acc, u_all.at[b], b, whole, t * half, half, True)
    for block in (sibling, across, diagonal):
        accumulate(acc, u_all.at[block], block, whole, t * half, half)
    m_copy(0).wait_recv()
    m_copy(2).start()
    m_copy(1).wait_recv()
    m_copy(2).wait_recv()
    square_stack[:rows, :], square_stack[rows:, :] = halves(square[...])
    for q in range(half // TILE):
        at = span(t * half + q * TILE, TILE)
        within = pl.ds(q * TILE, TILE)
        diag = alpha_part[:, :1] + beta_part[:, within]
        acc[:, at] = coef * acc[:, at] + product(square_stack[...], *halves(v_col[:, within])) + diag * v_all[b, :, at]
        own_copy(q).start()
    for q in range(half // TILE):
        own_copy(q).wait()
        f_copy(q).wait_recv()

    for q in range(half // TILE):
        f_copy(q).wait_send()
    for q in steps:
        z_copy(q, 1).wait_send()
        p_copy(q).wait_send()

        @pl.when(outer)
        def _():
            z_copy(q, 2).wait_send()

        @pl.when(inner)
        def _():
            z_copy(q, 3).wait_send()
            z_relay(q, 2).wait_send()
            z_relay(q, 3).wait_send()

    @pl.when(outer)
    def _():
        for n in range(3):
            e_copy(n).wait_send()

    @pl.when(inner)
    def _():
        for n in range(3, 6):
            e_copy(n).wait_send()

    a_copy().wait_send()
    a_relay().wait_send()
    for n in range(3):
        v_copy(n).wait_send()
        m_copy(n).wait_send()
        for piece_of in order:
            u_copy(n, *piece_of).wait_send()
    v_pass().wait_send()
    v_near().wait_send()
    for n in range(4):
        v_relay(n).wait_send()
    s_copy().wait_send()


def scratch(na, nb, rows, cols, full_a, alpha_size, beta_size):
    quarter = full_a // nb
    eighth = quarter // 2
    half = cols // 2
    buffers = [
        pltpu.VMEM((rows, full_a), F32),
        pltpu.VMEM((alpha_size // 128, 128), F32),
        pltpu.VMEM((beta_size // 128, 128), F32),
        pltpu.VMEM((2, STRIP, nb * cols), F32),
        pltpu.VMEM((cols, nb * cols), BF16),
        pltpu.VMEM((cols, nb * cols), BF16),
        pltpu.VMEM((nb, rows, cols), F32),
        pltpu.VMEM((full_a, half), F32),
        pltpu.VMEM((rows, full_a), F32),
        pltpu.VMEM((4 * rows, full_a), BF16),
        pltpu.VMEM((2 * rows, cols), BF16),
        pltpu.VMEM((rows, cols), F32),
        pltpu.VMEM((rows, cols), F32),
        pltpu.VMEM((rows, half), F32),
        pltpu.VMEM((rows, half), F32),
        pltpu.VMEM((rows, half), F32),
        pltpu.VMEM((nb, rows, cols), F32),
        pltpu.VMEM((eighth, full_a), F32),
        pltpu.VMEM((eighth, full_a), F32),
        pltpu.VMEM((2, eighth, rows), F32),
        pltpu.VMEM((2, eighth, rows), F32),
        pltpu.VMEM((eighth, rows), F32),
        pltpu.VMEM((eighth, rows), F32),
        pltpu.VMEM((rows, full_a), F32),
        pltpu.VMEM((2 * rows, full_a), BF16),
        pltpu.VMEM((rows, half), F32),
        pltpu.VMEM((rows, 128), F32),
        pltpu.VMEM((1, half), F32),
    ]
    dma = pltpu.SemaphoreType.DMA
    tiles = half // TILE
    parts = len(pieces_of(half))
    counts = [
        (max(4, tiles),), (2,), (parts, 3), (parts, 3), (parts, 2), (2,), (2,), (parts,), (parts,),
        (6,), (6,), (), (), (4,), (4,), (5,), (5,), (3, 2 * parts), (3, 2 * parts), (3,), (3,), (tiles,), (tiles,),
    ]
    return buffers, [dma(c) if c else dma for c in counts]


def fused(
    mesh, op_weight, vector, alpha_rows, beta_rows, alpha_string, beta_string, alpha_energy, beta_energy
):
    na, nb = mesh.shape["alpha"], mesh.shape["beta"]
    rows, cols = vector.shape
    buffers, semaphores = scratch(na, nb, rows, cols, alpha_rows.shape[1], alpha_energy.size, beta_energy.size)
    vmem = pl.BlockSpec(memory_space=pltpu.VMEM)
    whole = pl.BlockSpec(memory_space=pl.ANY)
    own, received = pl.pallas_call(
        functools.partial(kernel, na, nb),
        out_shape=[jax.ShapeDtypeStruct((rows, cols // 2), F32)] * 2,
        in_specs=[pl.BlockSpec(memory_space=pltpu.SMEM)] + [whole] * 4 + [vmem] * 2 + [whole],
        out_specs=[whole] * 2,
        scratch_shapes=buffers + semaphores,
        compiler_params=pltpu.CompilerParams(
            collective_id=0, has_side_effects=True, vmem_limit_bytes=60 * 1024 * 1024
        ),
    )(
        op_weight, vector, alpha_rows, alpha_energy.reshape(-1, 128), beta_energy.reshape(-1, 128),
        alpha_string.reshape(1, -1), beta_string.reshape(1, -1), beta_rows,
    )
    return own + received


def fits(mesh, vector, alpha_rows, alpha_energy, beta_energy):
    na, nb, nt = mesh.shape["alpha"], mesh.shape["beta"], mesh.shape["task"]
    rows, cols = vector.shape
    full_a = alpha_rows.shape[1]
    if nb != 4 or nt != 2 or na != 4 or cols % (8 * 128) or rows % 128 or full_a % (256 * nb) or full_a != na * rows:
        return False
    if alpha_energy.size % 128 or beta_energy.size % 128:
        return False
    buffers, _ = scratch(na, nb, rows, cols, full_a, alpha_energy.size, beta_energy.size)
    size = sum(buf.dtype.itemsize * functools.reduce(lambda x, y: x * y, buf.shape) for buf in buffers)
    size += 2 * rows * cols
    return size < VMEM_BUDGET


def collective(coefficient, vector, alpha_rows, beta_rows):
    high = lax.Precision.HIGH

    def dot(x, y):
        return jnp.dot(x, y, precision=high, preferred_element_type=F32)

    def apply_operator(block):
        left = dot(alpha_rows, lax.all_gather(block, "alpha", axis=0, tiled=True))
        return left + lax.psum_scatter(dot(block, beta_rows), "beta", scatter_dimension=1, tiled=True)

    second = apply_operator(apply_operator(vector))
    return lax.psum_scatter(coefficient * second, "task", scatter_dimension=1, tiled=True)


def on_device(
    mesh, vector, op_alpha, op_beta, op_weight, alpha_string, beta_string, alpha_energy, beta_energy
):
    if fits(mesh, vector, op_alpha[0], alpha_energy, beta_energy):
        return fused(
            mesh, op_weight, vector, op_alpha[0], op_beta[0],
            alpha_string, beta_string, alpha_energy, beta_energy,
        )
    task_index = lax.axis_index("task")
    summed = collective(0.5 * op_weight[task_index], vector, op_alpha[0], op_beta[0])
    width = summed.shape[1]
    column_start = task_index * width
    own_strings = lax.dynamic_slice_in_dim(beta_string, column_start, width, 0)
    own_vector = lax.dynamic_slice_in_dim(vector, column_start, width, 1)
    diag = alpha_energy[alpha_string][:, None] + beta_energy[own_strings][None, :]
    return summed + diag * own_vector


def solution(mesh):
    return jax.shard_map(
        functools.partial(on_device, mesh),
        mesh=mesh,
        in_specs=(
            P("alpha", "beta"),
            P("task", "alpha", None),
            P("task", "beta", None),
            P(),
            P("alpha"),
            P("beta"),
            P(),
            P(),
        ),
        out_specs=P("alpha", ("beta", "task")),
        check_vma=False,
    )
```
